32 devices in a mesh: dp: 8 (over y, x, core), tensor: 4 (over z).
Axes of the slice: x: 2, y: 2, z: 4, core: 2. Of those that a mesh axis runs over, the one named last changes fastest.
Arguments:
- block_in: bfloat16 [8192, 2048], P(('dp', 'tensor')), may hold values from -6 to 6
- slot_lengths: int32 [8], P('dp'), may hold values from 256 to 1024, as said below
- attn_gain: float32 [2048], replicated, may hold values from 0.5 to 1.5
- query_weight: bfloat16 [2048, 2048], P('dp', 'tensor'), may hold values from -0.125 to 0.125
- key_weight: bfloat16 [2048, 2048], P('dp', 'tensor'), may hold values from -0.125 to 0.125
- value_weight: bfloat16 [2048, 4096], P('dp', 'tensor'), may hold values from -0.125 to 0.125
- output_gate: bfloat16 [2048, 4096], P('dp', 'tensor'), may hold values from -0.125 to 0.125
- decay_weight: bfloat16 [2048, 16], P('dp', 'tensor'), may hold values from -0.125 to 0.125
- beta_weight: bfloat16 [2048, 16], P('dp', 'tensor'), may hold values from -0.125 to 0.125
- conv_weight: float32 [4, 8192], replicated, may hold values from -3 to 3
- decay_log: float32 [16], replicated, may hold values from -0.7 to 0.7
- step_bias: float32 [16], replicated, may hold values from -6.5 to -2
- head_gain: float32 [256], replicated, may hold values from 0.5 to 1.5
- out_weight: bfloat16 [4096, 2048], P('tensor', 'dp'), may hold values from -0.1875 to 0.1875
- ffn_gain: float32 [2048], replicated, may hold values from 0.5 to 1.5
- gate_weight: bfloat16 [2048, 5632], P('dp', 'tensor'), may hold values from -0.125 to 0.125
- up_weight: bfloat16 [2048, 5632], P('dp', 'tensor'), may hold values from -0.125 to 0.125
- down_weight: bfloat16 [5632, 2048], P('tensor', 'dp'), may hold values from -0.15625 to 0.15625
- out_grad: bfloat16 [8192, 2048], P(('dp', 'tensor')), may hold values from -6 to 6
Outputs:
- block_out: bfloat16 [8192, 2048], P(('dp', 'tensor'))
- grad_in: float32 [8192, 2048], P(('dp', 'tensor'))
- grad_attn_gain: float32 [2048], replicated
- grad_query: float32 [2048, 2048], P('dp', 'tensor')
- grad_key: float32 [2048, 2048], P('dp', 'tensor')
- grad_value: float32 [2048, 4096], P('dp', 'tensor')
- grad_output_gate: float32 [2048, 4096], P('dp', 'tensor')
- grad_decay: float32 [2048, 16], P('dp', 'tensor')
- grad_beta: float32 [2048, 16], P('dp', 'tensor')
- grad_conv: float32 [4, 8192], replicated
- grad_decay_log: float32 [16], replicated
- grad_step_bias: float32 [16], replicated
- grad_head_gain: float32 [256], replicated
- grad_out: float32 [4096, 2048], P('tensor', 'dp')
- grad_ffn_gain: float32 [2048], replicated
- grad_gate: float32 [2048, 5632], P('dp', 'tensor')
- grad_up: float32 [2048, 5632], P('dp', 'tensor')
- grad_down: float32 [5632, 2048], P('tensor', 'dp')
The draws below stay inside these ranges and needn't reach their ends.
Inputs may be any that keep to these rules, and one draw needn't show every extreme that they name: Slot s holds slot_lengths[s] live tokens from its first position on, the rest is padding; some slot is full.
All inputs are finite; a program needn't handle non-finite values.
Results may differ from the reference program's by a relative error of at most 0.011.
Values may be sent and summed in bfloat16 or wider, within the bound.
No kernel may reach another device: no remote copies, remote signals or barrier semaphores. Data moves between devices by JAX's collectives and lax.ppermute only.
A program may use at most 384 MiB of HBM per device.

```python
import jax
import jax.numpy as jnp
from jax import lax

D = 2048
HEADS = 16
DK = 128
DV = 256
FF = 5632
SPAN = 64
CONV = 4
SEQ_LEN = 1024
MIN_LEN = 256
SLOTS_DEV = 1
SLOTS = 8
TOKENS = 8192


def draw_slot_lengths(key, part):
    first_key, second_key = jax.random.split(jax.random.fold_in(key, 17), 2)
    lengths = jax.random.randint(first_key, (SLOTS,), MIN_LEN, SEQ_LEN + 1)
    chosen = jax.random.randint(second_key, (), 0, SLOTS)
    lengths = lengths.at[chosen].set(SEQ_LEN)
    return lengths.astype(jnp.int32)


def shard_levels(rng, dims, shards, least, high):
    def one(axis_at, blocks):
        draws = jax.random.uniform(jax.random.fold_in(jax.random.fold_in(rng, 6), axis_at), (blocks,), jnp.float32, least / len(shards), high / len(shards))
        return jnp.repeat(jnp.exp(draws), dims[axis_at] // blocks).reshape((-1,) + (1,) * (len(dims) - axis_at - 1))

    factor_of = one(*shards[0])
    for cut in shards[1:]:
        factor_of = factor_of * one(*cut)
    return factor_of


def scatter_about(stream_key, shape, deviation, reach, cuts=(), held_as=jnp.bfloat16):
    factor_of = shard_levels(stream_key, shape, cuts, -0.22, 0.18) if cuts else 1.0
    array = jax.random.normal(stream_key, shape, jnp.float32) * deviation * factor_of
    return jnp.minimum(jnp.maximum(array, -reach), reach).astype(held_as)


def setup_inputs(seed: int = 0) -> dict:
    seeds = jax.random.split(jax.random.key(seed), 20)
    return {
        "block_in": scatter_about(seeds[0], (TOKENS, D), 1.0, 6.0, ((0, 32),)),
        "slot_lengths": draw_slot_lengths(jax.random.fold_in(seeds[19], 71), 0),
        "attn_gain": jnp.clip(1.0 + 0.1 * jax.random.normal(seeds[2], (D,), jnp.float32), 0.5, 1.5),
        "query_weight": scatter_about(seeds[3], (D, HEADS * DK), D ** -0.5, 0.125, ((0, 8), (1, 4))),
        "key_weight": scatter_about(seeds[4], (D, HEADS * DK), D ** -0.5, 0.125, ((0, 8), (1, 4))),
        "value_weight": scatter_about(seeds[5], (D, HEADS * DV), D ** -0.5, 0.125, ((0, 8), (1, 4))),
        "output_gate": scatter_about(seeds[6], (D, HEADS * DV), D ** -0.5, 0.125, ((0, 8), (1, 4))),
        "decay_weight": scatter_about(seeds[7], (D, HEADS), D ** -0.5, 0.125, ((0, 8), (1, 4))),
        "beta_weight": scatter_about(seeds[8], (D, HEADS), D ** -0.5, 0.125, ((0, 8), (1, 4))),
        "conv_weight": scatter_about(seeds[9], (CONV, HEADS * (2 * DK + DV)), CONV ** -0.5, 3.0, (), jnp.float32),
        "decay_log": jnp.clip(jax.random.uniform(seeds[10], (HEADS,), jnp.float32, -0.7, 0.7), -0.7, 0.7),
        "step_bias": jnp.clip(jax.random.uniform(seeds[11], (HEADS,), jnp.float32, -6.5, -2.0), -6.5, -2.0),
        "head_gain": jnp.clip(1.0 + 0.1 * jax.random.normal(seeds[12], (DV,), jnp.float32), 0.5, 1.5),
        "out_weight": scatter_about(seeds[13], (HEADS * DV, D), (HEADS * DV // 4) ** -0.5, 0.1875, ((0, 4), (1, 8))),
        "ffn_gain": jnp.clip(1.0 + 0.1 * jax.random.normal(seeds[14], (D,), jnp.float32), 0.5, 1.5),
        "gate_weight": scatter_about(seeds[15], (D, FF), D ** -0.5, 0.125, ((0, 8), (1, 4))),
        "up_weight": scatter_about(seeds[16], (D, FF), D ** -0.5, 0.125, ((0, 8), (1, 4))),
        "down_weight": scatter_about(seeds[17], (FF, D), (FF // 4) ** -0.5, 0.15625, ((0, 4), (1, 8))),
        "out_grad": scatter_about(seeds[18], (TOKENS, D), 1.0, 6.0, ((0, 32),)),
    }


highest = lax.Precision.HIGHEST

@jax.custom_vjp
def low(v):
    return lax.optimization_barrier(v.astype(jnp.bfloat16)).astype(jnp.float32)

@jax.custom_vjp
def low_back(v):
    return v

def low_keep(v):
    return (low(v), None)

def low_pass(kept, grad):
    return (grad,)

def back_keep(v):
    return (v, None)

def back_low(kept, grad):
    return (low(grad),)
low.defvjp(low_keep, low_pass)
low_back.defvjp(back_keep, back_low)

def rms_norm(value_in, gain_in):
    scale_rows = lax.rsqrt(lax.optimization_barrier(jnp.mean(value_in * value_in, axis=-1, keepdims=True)) + 1e-05)
    return value_in * scale_rows * gain_in

def product(left_in, right_in):
    return jnp.dot(left_in, right_in, precision=highest, preferred_element_type=jnp.float32)

def short_conv(signal, weights):
    tap_count = weights.shape[0]
    length = signal.shape[1]
    padded = jnp.pad(signal, ((0, 0), (tap_count - 1, 0), (0, 0)))
    summed = jnp.zeros_like(signal)
    for offset in range(tap_count):
        summed = summed + padded[:, offset:offset + length, :] * weights[offset]
    return summed

def block_terms(queries, key_rows, value_rows, beta_rows, decay_rows):
    length = queries.shape[-2]
    row_ids = lax.broadcasted_iota(jnp.int32, (length, length), 0)
    col_ids = lax.broadcasted_iota(jnp.int32, (length, length), 1)
    strictly = row_ids > col_ids
    inclusive = row_ids >= col_ids
    cumulative = jnp.cumsum(decay_rows, axis=-1)
    spread = cumulative[..., :, None] - cumulative[..., None, :]
    lower_decay = jnp.where(strictly, jnp.exp(jnp.where(strictly, spread, 0.0)), 0.0)
    causal = jnp.where(inclusive, jnp.exp(jnp.where(inclusive, spread, 0.0)), 0.0)
    key_inner = jnp.einsum('nbhid,nbhjd->nbhij', key_rows, key_rows, precision=highest)
    nilpotent = beta_rows[..., :, None] * key_inner * lower_decay
    inverse = jnp.eye(length, dtype=jnp.float32) - nilpotent
    power = nilpotent
    for level in range((length - 1).bit_length() - 1):
        power = jnp.einsum('nbhij,nbhjk->nbhik', power, power, precision=highest)
        inverse = inverse + jnp.einsum('nbhij,nbhjk->nbhik', inverse, power, precision=highest)
    growth = jnp.exp(cumulative)
    targets = jnp.concatenate([(beta_rows * growth)[..., None] * key_rows, beta_rows[..., None] * value_rows], axis=-1)
    solved = jnp.einsum('nbhij,nbhje->nbhie', inverse, targets, precision=highest)
    key_width = key_rows.shape[-1]
    scores = jnp.einsum('nbhid,nbhjd->nbhij', queries, key_rows, precision=highest) * causal
    final_log = cumulative[..., -1:]
    carried = key_rows * jnp.exp(final_log - cumulative)[..., None]
    return (solved[..., :key_width], solved[..., key_width:], growth[..., None] * queries, scores, carried, jnp.exp(final_log))

def state_step(current, inputs):
    w_rows, u_rows, grown_queries, scores, carried, keep = inputs
    new_values = u_rows - jnp.einsum('bhcd,bhde->bhce', w_rows, current, precision=highest)
    output = jnp.einsum('bhcd,bhde->bhce', grown_queries, current, precision=highest)
    output = output + jnp.einsum('bhij,bhje->bhie', scores, new_values, precision=highest)
    current = keep[..., None] * current + jnp.einsum('bhcd,bhce->bhde', carried, new_values, precision=highest)
    return (current, output)

def mixer_core(query_proj, key_proj, value_proj, gate_proj, decay_proj, beta_proj, conv_taps, rate_log, bias_step, gain_head, token_mask=None, slot_count=1, block_length=64):
    tokens_all, key_channels = query_proj.shape
    heads_here = decay_proj.shape[1]
    key_width = key_channels // heads_here
    value_width = value_proj.shape[1] // heads_here
    slot_length = tokens_all // slot_count
    joined = jnp.concatenate([query_proj, key_proj, value_proj], axis=1).reshape(slot_count, slot_length, -1)
    convolved = jax.nn.silu(short_conv(joined, conv_taps))
    queries = convolved[..., :key_channels].reshape(slot_count, slot_length, heads_here, key_width)
    key_rows = convolved[..., key_channels:2 * key_channels].reshape(slot_count, slot_length, heads_here, key_width)
    value_rows = convolved[..., 2 * key_channels:].reshape(slot_count, slot_length, heads_here, value_width)
    queries = queries * lax.rsqrt(lax.optimization_barrier(jnp.sum(queries * queries, axis=-1, keepdims=True)) + 1e-06) * key_width ** (-0.5)
    key_rows = key_rows * lax.rsqrt(lax.optimization_barrier(jnp.sum(key_rows * key_rows, axis=-1, keepdims=True)) + 1e-06)
    mask_rows = token_mask.reshape(slot_count, slot_length, 1)
    beta_rows = jax.nn.sigmoid(beta_proj.reshape(slot_count, slot_length, heads_here)) * mask_rows
    decay_rows = -jnp.exp(rate_log) * jax.nn.softplus(decay_proj.reshape(slot_count, slot_length, heads_here) + bias_step)
    blocks = slot_length // block_length

    def to_blocks(source):
        shaped = source.reshape((slot_count, blocks, block_length) + source.shape[2:])
        return jnp.moveaxis(jnp.moveaxis(shaped, 1, 0), 3, 2)
    terms = jax.checkpoint(block_terms)(to_blocks(queries), to_blocks(key_rows), to_blocks(value_rows), to_blocks(beta_rows), to_blocks(decay_rows))
    initial = jnp.zeros((slot_count, heads_here, key_width, value_width), jnp.float32)
    _, outputs = lax.scan(jax.checkpoint(state_step), initial, terms)
    outputs = jnp.moveaxis(jnp.moveaxis(outputs, 3, 2), 0, 1).reshape(tokens_all, heads_here, value_width)
    normed = outputs * lax.rsqrt(lax.optimization_barrier(jnp.mean(outputs * outputs, axis=-1, keepdims=True)) + 1e-05) * gain_head
    gated = normed * jax.nn.silu(gate_proj.reshape(tokens_all, heads_here, value_width))
    return gated.reshape(tokens_all, heads_here * value_width)

def block_forward(inputs, token_mask, attn_gain, query_weight, key_weight, value_weight, output_gate, decay_weight, beta_weight, conv_weight, decay_log, step_bias, head_gain, out_weight, ffn_gain, gate_weight, up_weight, down_weight):
    mixer_in = low(rms_norm(inputs, attn_gain))
    query_proj = low_back(product(mixer_in, query_weight))
    key_proj = low_back(product(mixer_in, key_weight))
    value_proj = low_back(product(mixer_in, value_weight))
    gate_proj = low_back(product(mixer_in, output_gate))
    decay_proj = low_back(product(mixer_in, decay_weight))
    beta_proj = low_back(product(mixer_in, beta_weight))
    gated = mixer_core(query_proj, key_proj, value_proj, gate_proj, decay_proj, beta_proj, conv_weight, decay_log, step_bias, head_gain, token_mask=token_mask, slot_count=SLOTS_DEV, block_length=SPAN)
    mixer_out = low_back(product(low(gated), out_weight))
    hidden = inputs + mixer_out
    ffn_in = low(rms_norm(hidden, ffn_gain))
    gate_act = low_back(product(ffn_in, gate_weight))
    up_act = low_back(product(ffn_in, up_weight))
    inner_act = low(jax.nn.silu(gate_act) * up_act)
    ffn_out = low_back(product(inner_act, down_weight))
    return token_mask[:, None] * (hidden + ffn_out)

def reference(block_in, slot_lengths, attn_gain, query_weight, key_weight, value_weight, output_gate, decay_weight, beta_weight, conv_weight, decay_log, step_bias, head_gain, out_weight, ffn_gain, gate_weight, up_weight, down_weight, out_grad):
    groups = SLOTS // SLOTS_DEV
    positions = jnp.arange(SEQ_LEN, dtype=jnp.int32)
    token_mask = (positions[None, :] < slot_lengths[:, None]).astype(jnp.float32).reshape(groups, SLOTS_DEV * SEQ_LEN)
    rows_in = block_in.astype(jnp.float32).reshape(groups, SLOTS_DEV * SEQ_LEN, D)
    params = tuple((weight_arg.astype(jnp.float32) for weight_arg in (attn_gain, query_weight, key_weight, value_weight, output_gate, decay_weight, beta_weight, conv_weight, decay_log, step_bias, head_gain, out_weight, ffn_gain, gate_weight, up_weight, down_weight)))

    def whole(rows_all, weights):

        def one_group(paired):
            return block_forward(paired[0], paired[1], *weights)
        return lax.map(jax.checkpoint(one_group), (rows_all, token_mask))
    result, pullback = jax.vjp(whole, rows_in, params)
    grads_in, grads_w = pullback(out_grad.astype(jnp.float32).reshape(groups, SLOTS_DEV * SEQ_LEN, D))
    return (result.reshape(TOKENS, D).astype(jnp.bfloat16), grads_in.reshape(TOKENS, D), grads_w[0], grads_w[1], grads_w[2], grads_w[3], grads_w[4], grads_w[5], grads_w[6], grads_w[7], grads_w[8], grads_w[9], grads_w[10], grads_w[11], grads_w[12], grads_w[13], grads_w[14], grads_w[15])
```

```python
import functools

import jax
import jax.numpy as jnp
from jax import lax
from jax.experimental import pallas as pl
from jax.experimental.pallas import tpu as pltpu
from jax.sharding import PartitionSpec as P

f32, bf16 = jnp.float32, jnp.bfloat16
HALO = 8
LANES = 128


def contract(left_in, right_in, left_dim, right_dim):
    return lax.dot_general(
        left_in, right_in, (((left_dim,), (right_dim,)), ((), ())), preferred_element_type=f32
    )


def dot_low(left_in, right_in, left_dim, right_dim):
    return contract(left_in.astype(bf16), right_in.astype(bf16), left_dim, right_dim)


def two_terms(value_in):
    high = value_in.astype(bf16)
    return high, (value_in - high.astype(f32)).astype(bf16)


def dot_split(left_in, right_in, left_dim, right_dim):
    (lh, ll), (rh, rl) = left_in, right_in
    return (
        contract(lh, rh, left_dim, right_dim)
        + contract(lh, rl, left_dim, right_dim)
        + contract(ll, rh, left_dim, right_dim)
    )


def sigmoid(value_in):
    return 1.0 / (1.0 + jnp.exp(-value_in))


def block_inverse(terms, base):
    size = terms[0].shape[0]
    rows = lax.broadcasted_iota(jnp.int32, (size, size), 0)
    cols = lax.broadcasted_iota(jnp.int32, (size, size), 1)
    eye = (rows == cols).astype(f32)
    near = (rows // base) == (cols // base)
    diag = [jnp.where(near, a, 0.0) for a in terms]
    off = [jnp.where(near, 0.0, a) for a in terms]
    power = diag
    inv = [eye - a for a in diag]
    for _ in range(base.bit_length() - 2):
        power = [dot_low(p, p, 1, 0) for p in power]
        inv = [x + dot_low(x, p, 1, 0) for x, p in zip(inv, power)]
    if size == base:
        return inv
    step = [dot_low(x, e, 1, 0) for x, e in zip(inv, off)]
    outer = [eye - n for n in step]
    power = step
    for _ in range((size // base).bit_length() - 2):
        power = [dot_low(p, p, 1, 0) for p in power]
        outer = [y + dot_low(y, p, 1, 0) for y, p in zip(outer, power)]
    return [dot_low(y, x, 1, 0) for y, x in zip(outer, inv)]


def small_terms(small, rate_row, bias_row, mask_col, heads, size):
    z = small + bias_row
    soft = jnp.maximum(z, 0.0) + jnp.log(1.0 + jnp.exp(-jnp.abs(z)))
    decay = -jnp.exp(rate_row) * soft
    rows = lax.broadcasted_iota(jnp.int32, (size, size), 0)
    cols = lax.broadcasted_iota(jnp.int32, (size, size), 1)
    tril = (rows >= cols).astype(bf16)
    hi, lo = two_terms(decay)
    lo2 = (decay - hi.astype(f32) - lo.astype(f32)).astype(bf16)
    cum = contract(tril, hi, 1, 0) + contract(tril, lo, 1, 0) + contract(tril, lo2, 1, 0)
    beta = sigmoid(small) * mask_col
    return z, decay, cum, beta


def conv_rows(ext_ref, taps_ref, size):
    total = None
    count = taps_ref.shape[0]
    for j in range(count):
        term = ext_ref[pl.ds(HALO - count + 1 + j, size), :] * taps_ref[pl.ds(j, 1), :]
        total = term if total is None else total + term
    return total


def unit_rows(pre, scale):
    sig = sigmoid(pre)
    y = pre * sig
    r = lax.rsqrt(jnp.sum(y * y, axis=-1, keepdims=True) + 1e-06)
    return sig, r, y * r


def mixer_forward_kernel(
    heads, kw, vw, size, base,
    len_ref, proj_ref, halo_ref, taps_ref, par_ref, gain_ref,
    gated_ref, o_ref, x_ref, new_ref, s_ref,
    ext_ref, pre_ref, state_ref,
):
    slot, blk = pl.program_id(0), pl.program_id(1)
    conv_width = heads * (2 * kw + vw)
    gate_at, small_at = conv_width, conv_width + heads * vw

    @pl.when(blk == 0)
    def _():
        state_ref[...] = jnp.zeros_like(state_ref)

    ext_ref[pl.ds(0, HALO), :] = jnp.where(blk > 0, halo_ref[...], 0.0)
    ext_ref[pl.ds(HALO, size), :] = proj_ref[:, :conv_width]
    pre_ref[...] = conv_rows(ext_ref, taps_ref, size)
    pos = blk * size + lax.broadcasted_iota(jnp.int32, (size, 1), 0)
    mask_col = (pos < len_ref[slot]).astype(f32)
    small = proj_ref[:, small_at : small_at + 128]
    _, _, cum, beta = small_terms(small, par_ref[0:1, :], par_ref[1:2, :], mask_col, heads, size)
    cum_t = cum.T
    rows = lax.broadcasted_iota(jnp.int32, (size, size), 0)
    cols = lax.broadcasted_iota(jnp.int32, (size, size), 1)
    hs = range(heads)
    scale = kw ** (-0.5)
    q, k, v = [], [], []
    for h in hs:
        _, _, u = unit_rows(pre_ref[:, h * kw : (h + 1) * kw], 1.0)
        q.append((u * scale).astype(bf16))
        _, _, u = unit_rows(pre_ref[:, (heads + h) * kw : (heads + h + 1) * kw], 1.0)
        k.append(u)
        pv = pre_ref[:, 2 * heads * kw + h * vw : 2 * heads * kw + (h + 1) * vw]
        v.append(pv * sigmoid(pv))
    kl = [a.astype(bf16) for a in k]
    cc = [cum[:, h : h + 1] for h in hs]
    cr = [cum_t[h : h + 1, :] for h in hs]
    bc = [beta[:, heads + h : heads + h + 1] for h in hs]
    dec = [jnp.where(rows >= cols, jnp.exp(jnp.minimum(cc[h] - cr[h], 0.0)), 0.0) for h in hs]
    kk = [contract(kl[h], kl[h], 1, 1) for h in hs]
    qk = [contract(q[h], kl[h], 1, 1) for h in hs]
    a = [jnp.where(rows > cols, bc[h] * kk[h] * dec[h], 0.0) for h in hs]
    inv = block_inverse(a, base)
    sl = [state_ref[h].astype(bf16) for h in hs]
    ks = [contract(kl[h], sl[h], 1, 0) for h in hs]
    qs = [contract(q[h], sl[h], 1, 0) for h in hs]
    ec = [jnp.exp(cc[h]) for h in hs]
    rhs = [bc[h] * (v[h] - ec[h] * ks[h]) for h in hs]
    new = [dot_split(two_terms(inv[h]), two_terms(rhs[h]), 1, 0) for h in hs]
    new2 = [two_terms(new[h]) for h in hs]
    o = [ec[h] * qs[h] + dot_split(two_terms(qk[h] * dec[h]), new2[h], 1, 0) for h in hs]
    for h in hs:
        s_ref[0, h] = state_ref[h]
        last = cum[size - 1 : size, h : h + 1]
        kel = (k[h] * jnp.exp(last - cc[h])).astype(bf16)
        state_ref[h] = jnp.exp(last) * state_ref[h] + contract(kel, new2[h][0], 0, 0)
        x_ref[:, h * size : (h + 1) * size] = inv[h]
        new_ref[:, h * vw : (h + 1) * vw] = new[h]
        o_ref[:, h * vw : (h + 1) * vw] = o[h]
        r = lax.rsqrt(jnp.mean(o[h] * o[h], axis=-1, keepdims=True) + 1e-05)
        g = proj_ref[:, gate_at + h * vw : gate_at + (h + 1) * vw]
        gated_ref[:, h * vw : (h + 1) * vw] = (
            o[h] * r * gain_ref[...] * (g * sigmoid(g))
        ).astype(bf16)


def mixer_backward_kernel(
    heads, kw, vw, size, base,
    len_ref, proj_ref, halo_ref, taps_ref, par_ref, gain_ref, dg_ref, o_ref, x_ref, new_ref, s_ref,
    dproj_ref, dtaps_ref, dpar_ref, dgain_ref,
    ext_ref, pre_ref, dext_ref, dstate_ref,
):
    slot, step = pl.program_id(0), pl.program_id(1)
    blk = pl.num_programs(1) - 1 - step
    conv_width = heads * (2 * kw + vw)
    gate_at, small_at = conv_width, conv_width + heads * vw
    count = taps_ref.shape[0]

    @pl.when((step == 0) & (slot == 0))
    def _():
        dtaps_ref[...] = jnp.zeros_like(dtaps_ref)
        dpar_ref[...] = jnp.zeros_like(dpar_ref)
        dgain_ref[...] = jnp.zeros_like(dgain_ref)

    @pl.when(step == 0)
    def _():
        dstate_ref[...] = jnp.zeros_like(dstate_ref)
        dext_ref[pl.ds(0, HALO), :] = jnp.zeros((HALO, conv_width), f32)

    dext_ref[pl.ds(size, HALO), :] = dext_ref[pl.ds(0, HALO), :]
    ext_ref[pl.ds(0, HALO), :] = jnp.where(blk > 0, halo_ref[...], 0.0)
    ext_ref[pl.ds(HALO, size), :] = proj_ref[:, :conv_width]
    pre_ref[...] = conv_rows(ext_ref, taps_ref, size)
    pos = blk * size + lax.broadcasted_iota(jnp.int32, (size, 1), 0)
    mask_col = (pos < len_ref[slot]).astype(f32)
    small = proj_ref[:, small_at : small_at + 128]
    z, decay, cum, beta = small_terms(small, par_ref[0:1, :], par_ref[1:2, :], mask_col, heads, size)
    cum_t = cum.T
    rows = lax.broadcasted_iota(jnp.int32, (size, size), 0)
    cols = lax.broadcasted_iota(jnp.int32, (size, size), 1)
    hs = range(heads)
    scale = kw ** (-0.5)
    at_q = [slice(h * kw, (h + 1) * kw) for h in hs]
    at_k = [slice((heads + h) * kw, (heads + h + 1) * kw) for h in hs]
    at_v = [slice(2 * heads * kw + h * vw, 2 * heads * kw + (h + 1) * vw) for h in hs]
    at_o = [slice(h * vw, (h + 1) * vw) for h in hs]
    do, ec = [], []
    cc = [cum[:, h : h + 1] for h in hs]
    cr = [cum_t[h : h + 1, :] for h in hs]
    bc = [beta[:, heads + h : heads + h + 1] for h in hs]
    dgain = jnp.zeros((1, vw), f32)
    for h in hs:
        g = proj_ref[:, gate_at + h * vw : gate_at + (h + 1) * vw]
        sg = sigmoid(g)
        silu = g * sg
        o = o_ref[:, at_o[h]]
        r = lax.rsqrt(jnp.mean(o * o, axis=-1, keepdims=True) + 1e-05)
        on = o * r
        dg = dg_ref[:, at_o[h]]
        both = dg * on
        dproj_ref[:, gate_at + h * vw : gate_at + (h + 1) * vw] = (
            both * gain_ref[...] * (sg * (1.0 + g * (1.0 - sg)))
        ).astype(bf16)
        dgain = dgain + jnp.sum(both * silu, axis=0, keepdims=True)
        don = dg * gain_ref[...] * silu
        do.append(r * (don - on * jnp.mean(on * don, axis=-1, keepdims=True)))
        ec.append(jnp.exp(cc[h]))
    dgain_ref[...] += dgain
    q, k, ql, kl = [], [], [], []
    for h in hs:
        _, _, u = unit_rows(pre_ref[:, at_q[h]], 1.0)
        q.append(u * scale)
        _, _, u = unit_rows(pre_ref[:, at_k[h]], 1.0)
        k.append(u)
    ql = [u.astype(bf16) for u in q]
    kl = [u.astype(bf16) for u in k]
    dec = [jnp.where(rows >= cols, jnp.exp(jnp.minimum(cc[h] - cr[h], 0.0)), 0.0) for h in hs]
    kk = [contract(kl[h], kl[h], 1, 1) for h in hs]
    qk = [contract(ql[h], kl[h], 1, 1) for h in hs]
    pm = [qk[h] * dec[h] for h in hs]
    sl = [s_ref[0, h].astype(bf16) for h in hs]
    tl = [dstate_ref[h].astype(bf16) for h in hs]
    ks = [contract(kl[h], sl[h], 1, 0) for h in hs]
    qs = [contract(ql[h], sl[h], 1, 0) for h in hs]
    new2 = [two_terms(new_ref[:, at_o[h]]) for h in hs]
    do2 = [two_terms(do[h]) for h in hs]
    last = [cum[size - 1 : size, h : h + 1] for h in hs]
    el = [jnp.exp(last[h] - cc[h]) for h in hs]
    kel = [(k[h] * el[h]).astype(bf16) for h in hs]
    dpm = [dot_split(do2[h], new2[h], 1, 1) for h in hs]
    dnew = [dot_split(two_terms(pm[h]), do2[h], 0, 0) + contract(kel[h], tl[h], 1, 0) for h in hs]
    drhs = [dot_split(two_terms(x_ref[:, h * size : (h + 1) * size]), two_terms(dnew[h]), 0, 0) for h in hs]
    da = [-dot_split(two_terms(drhs[h]), new2[h], 1, 1) for h in hs]
    dkel = [contract(new2[h][0], tl[h], 1, 1) for h in hs]
    dcol, dbeta = [], []
    dq, dk, edo, edz = [], [], [], []
    lastrow = (lax.broadcasted_iota(jnp.int32, (size, 1), 0) == size - 1).astype(f32)
    for h in hs:
        pv = pre_ref[:, at_v[h]]
        sv = sigmoid(pv)
        zz = pv * sv - ec[h] * ks[h]
        dz = bc[h] * drhs[h]
        db = jnp.sum(drhs[h] * zz, axis=-1, keepdims=True)
        dext_ref[pl.ds(0, size), at_v[h]] = dz * (sv * (1.0 + pv * (1.0 - sv)))
        edo.append((ec[h] * do[h]).astype(bf16))
        edz.append((-ec[h] * dz).astype(bf16))
        dec_col = jnp.sum(do[h] * qs[h] - dz * ks[h], axis=-1, keepdims=True)
        dam = jnp.where(rows > cols, da[h], 0.0)
        dpmm = jnp.where(rows >= cols, dpm[h], 0.0)
        kd = kk[h] * dec[h]
        db = db + jnp.sum(dam * kd, axis=-1, keepdims=True)
        dspread = dpmm * pm[h] + dam * (bc[h] * kd)
        dqk = (dpmm * dec[h]).astype(bf16)
        dkk = (dam * (bc[h] * dec[h])).astype(bf16)
        d_el = jnp.sum(dkel[h] * k[h], axis=-1, keepdims=True) * el[h]
        d_keep = jnp.sum(jnp.sum(dstate_ref[h] * s_ref[0, h], axis=-1, keepdims=True), axis=0, keepdims=True)
        d_last = d_keep * jnp.exp(last[h]) + jnp.sum(d_el, axis=0, keepdims=True)
        col = jnp.sum(dspread, axis=-1, keepdims=True) + dec_col * ec[h] - d_el + lastrow * d_last
        row = jnp.sum(dspread, axis=0, keepdims=True)
        dcol.append((col, row))
        dbeta.append(db)
        dq.append(contract(edo[h], sl[h], 1, 1) + contract(dqk, kl[h], 1, 0))
        dk.append(
            contract(edz[h], sl[h], 1, 1)
            + dkel[h] * el[h]
            + contract(dqk, ql[h], 0, 0)
            + contract(dkk, kl[h], 1, 0)
            + contract(dkk, kl[h], 0, 0)
        )
    for h in hs:
        dstate_ref[h] = (
            jnp.exp(last[h]) * dstate_ref[h]
            + contract(ql[h], edo[h], 0, 0)
            + contract(kl[h], edz[h], 0, 0)
        )
        for at, grad, fac in ((at_q[h], dq[h], scale), (at_k[h], dk[h], 1.0)):
            pre = pre_ref[:, at]
            sig, r, u = unit_rows(pre, 1.0)
            du = grad * fac
            dy = r * (du - u * jnp.sum(u * du, axis=-1, keepdims=True))
            dext_ref[pl.ds(0, size), at] = dy * (sig * (1.0 + pre * (1.0 - sig)))
    lanes = lax.broadcasted_iota(jnp.int32, (size, 128), 1)
    subs = lax.broadcasted_iota(jnp.int32, (128, size), 0)
    dcum = jnp.zeros((size, 128), f32)
    drow = jnp.zeros((128, size), f32)
    dbeta_all = jnp.zeros((size, 128), f32)
    for h in hs:
        dcum = jnp.where(lanes == h, dcol[h][0], dcum)
        drow = jnp.where(subs == h, dcol[h][1], drow)
        dbeta_all = jnp.where(lanes == heads + h, dbeta[h], dbeta_all)
    dcum = dcum - drow.T
    triu = (rows <= cols).astype(bf16)
    hi, lo = two_terms(dcum)
    ddecay = contract(triu, hi, 1, 0) + contract(triu, lo, 1, 0)
    dz = ddecay * (-jnp.exp(par_ref[0:1, :])) * sigmoid(z)
    dpar_ref[0:1, :] += jnp.sum(ddecay * decay, axis=0, keepdims=True)
    dpar_ref[1:2, :] += jnp.sum(dz, axis=0, keepdims=True)
    sb = sigmoid(small)
    dsmall = dz + dbeta_all * mask_col * sb * (1.0 - sb)
    dproj_ref[:, small_at : small_at + 128] = dsmall.astype(bf16)
    dpre = dext_ref[pl.ds(0, size), :]
    total = None
    for j in range(count):
        back = dext_ref[pl.ds(count - 1 - j, size), :] * taps_ref[pl.ds(j, 1), :]
        total = back if total is None else total + back
        seen = ext_ref[pl.ds(HALO - count + 1 + j, size), :]
        dtaps_ref[pl.ds(j, 1), :] += jnp.sum(dpre * seen, axis=0, keepdims=True)
    dproj_ref[:, :conv_width] = total.astype(bf16)


def mixer_specs(heads, kw, vw, size, blocks, width, taps, order):
    conv_width = heads * (2 * kw + vw)
    per = size // HALO
    at = lambda s, b, *_: (s * blocks + order(b), 0)
    return dict(
        proj=pl.BlockSpec((size, width), at),
        halo=pl.BlockSpec(
            (HALO, conv_width),
            lambda s, b, *_: (jnp.maximum((s * blocks + order(b)) * per - 1, 0), 0),
        ),
        taps=pl.BlockSpec((taps, conv_width), lambda s, b, *_: (0, 0)),
        par=pl.BlockSpec((8, 128), lambda s, b, *_: (0, 0)),
        gain=pl.BlockSpec((1, vw), lambda s, b, *_: (0, 0)),
        value=pl.BlockSpec((size, heads * vw), at),
        inv=pl.BlockSpec((size, heads * size), at),
        state=pl.BlockSpec((1, heads, kw, vw), lambda s, b, *_: (s * blocks + order(b), 0, 0, 0)),
    )


def mixer_forward(lengths, proj, taps, par, gain, heads, kw, vw, size=128, base=16):
    slots = lengths.shape[0]
    rows, width = proj.shape
    blocks = rows // slots // size
    sp = mixer_specs(heads, kw, vw, size, blocks, width, taps.shape[0], lambda b: b)
    conv_width = heads * (2 * kw + vw)
    return pl.pallas_call(
        functools.partial(mixer_forward_kernel, heads, kw, vw, size, base),
        grid_spec=pltpu.PrefetchScalarGridSpec(
            num_scalar_prefetch=1,
            grid=(slots, blocks),
            in_specs=[sp["proj"], sp["halo"], sp["taps"], sp["par"], sp["gain"]],
            out_specs=[sp["value"], sp["value"], sp["inv"], sp["value"], sp["state"]],
            scratch_shapes=[
                pltpu.VMEM((size + HALO, conv_width), f32),
                pltpu.VMEM((size, conv_width), f32),
                pltpu.VMEM((heads, kw, vw), f32),
            ],
        ),
        out_shape=[
            jax.ShapeDtypeStruct((rows, heads * vw), bf16),
            jax.ShapeDtypeStruct((rows, heads * vw), f32),
            jax.ShapeDtypeStruct((rows, heads * size), f32),
            jax.ShapeDtypeStruct((rows, heads * vw), f32),
            jax.ShapeDtypeStruct((slots * blocks, heads, kw, vw), f32),
        ],
        compiler_params=pltpu.CompilerParams(dimension_semantics=("arbitrary", "arbitrary")),
        name="mixer_forward",
    )(lengths, proj, proj, taps, par, gain)


def mixer_backward(lengths, proj, taps, par, gain, dgated, o, inv, new, state, heads, kw, vw, size=128, base=16):
    slots = lengths.shape[0]
    rows, width = proj.shape
    blocks = rows // slots // size
    sp = mixer_specs(heads, kw, vw, size, blocks, width, taps.shape[0], lambda b: blocks - 1 - b)
    conv_width = heads * (2 * kw + vw)
    return pl.pallas_call(
        functools.partial(mixer_backward_kernel, heads, kw, vw, size, base),
        grid_spec=pltpu.PrefetchScalarGridSpec(
            num_scalar_prefetch=1,
            grid=(slots, blocks),
            in_specs=[sp["proj"], sp["halo"], sp["taps"], sp["par"], sp["gain"], sp["value"], sp["value"], sp["inv"], sp["value"], sp["state"]],
            out_specs=[sp["proj"], sp["taps"], sp["par"], sp["gain"]],
            scratch_shapes=[
                pltpu.VMEM((size + HALO, conv_width), f32),
                pltpu.VMEM((size, conv_width), f32),
                pltpu.VMEM((size + HALO, conv_width), f32),
                pltpu.VMEM((heads, kw, vw), f32),
            ],
        ),
        out_shape=[
            jax.ShapeDtypeStruct((rows, width), bf16),
            jax.ShapeDtypeStruct(taps.shape, f32),
            jax.ShapeDtypeStruct((8, 128), f32),
            jax.ShapeDtypeStruct((1, vw), f32),
        ],
        compiler_params=pltpu.CompilerParams(dimension_semantics=("arbitrary", "arbitrary")),
        name="mixer_backward",
    )(lengths, proj, proj, taps, par, gain, dgated, o, inv, new, state)


def line_steps(size):
    return [(i, i + 1) for i in range(size - 1)], [(i + 1, i) for i in range(size - 1)]


def line_gather(piece, axis):
    size = lax.axis_size(axis)
    me = lax.axis_index(axis)
    up, down = line_steps(size)
    below, above = [], []
    a = b = piece
    for _ in range(size - 1):
        a = lax.ppermute(a, axis, up)
        b = lax.ppermute(b, axis, down)
        below.insert(0, a)
        above.append(b)
    rows = piece.shape[0]
    joined = jnp.concatenate(below + [piece] + above, axis=0)
    return lax.dynamic_slice_in_dim(joined, (size - 1 - me) * rows, size * rows, 0)


def line_scatter(parts, axis):
    size = lax.axis_size(axis)
    me = lax.axis_index(axis)
    rows = parts.shape[0] // size

    def owned(index):
        return lax.dynamic_slice_in_dim(parts, lax.rem(index + 2 * size, size) * rows, rows, 0)

    from_below = from_above = None
    for step in range(1, size):
        send = owned(me - step)
        if from_below is not None:
            send = send + from_below.astype(f32)
        from_below = lax.ppermute(
            send.astype(bf16), axis, [(i, i + 1) for i in range(min(step, size - 1))]
        )
        send = owned(me + step)
        if from_above is not None:
            send = send + from_above.astype(f32)
        from_above = lax.ppermute(
            send.astype(bf16), axis, [(size - 1 - i, size - 2 - i) for i in range(min(step, size - 1))]
        )
    return owned(me) + from_below.astype(f32) + from_above.astype(f32)


def cube_sum(value_in, axis):
    size = lax.axis_size(axis)
    if size & (size - 1):
        return lax.psum(value_in, axis)
    bit = 1
    while bit < size:
        value_in = value_in + lax.ppermute(value_in, axis, [(i, i ^ bit) for i in range(size)])
        bit *= 2
    return value_in


def rms_rows(value_in):
    return lax.rsqrt(jnp.mean(value_in * value_in, axis=-1, keepdims=True) + 1e-05)


def body(
    block_in,
    slot_lengths,
    attn_gain,
    query_weight,
    key_weight,
    value_weight,
    output_gate,
    decay_weight,
    beta_weight,
    conv_weight,
    decay_log,
    step_bias,
    head_gain,
    out_weight,
    ffn_gain,
    gate_weight,
    up_weight,
    down_weight,
    out_grad,
):
    tensor_size = lax.axis_size("tensor")
    tensor_rank = lax.axis_index("tensor")
    local_rows = block_in.shape[0]
    group_rows = local_rows * tensor_size
    slots_here = slot_lengths.shape[0]
    slot_length = group_rows // slots_here
    heads_here = decay_weight.shape[1]
    total_heads = decay_log.shape[0]
    key_channels = query_weight.shape[1]
    value_channels = value_weight.shape[1]
    key_width = key_channels // heads_here
    value_width = value_channels // heads_here
    positions = jnp.arange(slot_length, dtype=jnp.int32)
    group_mask = (
        (positions[None, :] < slot_lengths[:, None]).astype(f32).reshape(group_rows)
    )
    local_mask = lax.dynamic_slice_in_dim(group_mask, tensor_rank * local_rows, local_rows)[:, None]
    query_start = tensor_rank * key_channels
    key_start = total_heads * key_width + tensor_rank * key_channels
    value_start = 2 * total_heads * key_width + tensor_rank * value_channels
    taps = jnp.concatenate(
        [
            lax.dynamic_slice_in_dim(conv_weight, query_start, key_channels, 1),
            lax.dynamic_slice_in_dim(conv_weight, key_start, key_channels, 1),
            lax.dynamic_slice_in_dim(conv_weight, value_start, value_channels, 1),
        ],
        axis=1,
    )
    rate_local = lax.dynamic_slice_in_dim(decay_log, tensor_rank * heads_here, heads_here)
    bias_local = lax.dynamic_slice_in_dim(step_bias, tensor_rank * heads_here, heads_here)
    par = jnp.pad(jnp.stack([rate_local, bias_local]), ((0, 6), (0, LANES - heads_here)))
    gain_row = head_gain[None, :]

    small_local = jnp.concatenate([decay_weight, beta_weight], axis=1)
    mix_local = jnp.concatenate(
        [
            query_weight,
            key_weight,
            value_weight,
            output_gate,
            jnp.pad(small_local, ((0, 0), (0, LANES - 2 * heads_here))),
        ],
        axis=1,
    )
    mix_full = lax.all_gather(mix_local, "dp", axis=0, tiled=True)
    out_full = lax.all_gather(out_weight, "dp", axis=1, tiled=True)
    gate_full = lax.all_gather(gate_weight, "dp", axis=0, tiled=True)
    up_full = lax.all_gather(up_weight, "dp", axis=0, tiled=True)
    down_full = lax.all_gather(down_weight, "dp", axis=1, tiled=True)

    block_rows = block_in.astype(f32)
    block_full = line_gather(block_in, "tensor").astype(f32)
    block_unit = block_full * rms_rows(block_full)
    mixer_rows = (block_unit * attn_gain).astype(bf16)
    proj = jnp.dot(mixer_rows, mix_full, preferred_element_type=f32)
    gated, o, inv, new, state = mixer_forward(
        slot_lengths, proj, taps, par, gain_row, heads_here, key_width, value_width
    )
    mixer_out = line_scatter(jnp.dot(gated, out_full, preferred_element_type=f32), "tensor")
    hidden = block_rows + mixer_out
    hidden_scale = rms_rows(hidden)
    hidden_unit = hidden * hidden_scale
    ffn_rows = line_gather((hidden_unit * ffn_gain).astype(bf16), "tensor")

    gate_act = jnp.dot(ffn_rows, gate_full, preferred_element_type=f32)
    up_act = jnp.dot(ffn_rows, up_full, preferred_element_type=f32)
    gate_sig = jax.nn.sigmoid(gate_act)
    gate_silu = gate_act * gate_sig
    inner_low = (gate_silu * up_act).astype(bf16)
    out_masked = out_grad.astype(f32) * local_mask
    back_rows = line_gather(out_masked.astype(bf16), "tensor")
    d_inner = contract(back_rows, down_full, 1, 1)
    d_gate = (d_inner * up_act * gate_sig * (1.0 + gate_act * (1.0 - gate_sig))).astype(bf16)
    d_up = (d_inner * gate_silu).astype(bf16)
    ffn_part = contract(d_gate, gate_full, 1, 1) + contract(d_up, up_full, 1, 1)
    d_ffn_in = line_scatter(ffn_part, "tensor")
    grad_ffn_gain = jnp.sum(d_ffn_in * hidden_unit, axis=0)
    dn = d_ffn_in * ffn_gain
    d_hidden = out_masked + hidden_scale * (
        dn - hidden_unit * jnp.mean(dn * hidden_unit, axis=-1, keepdims=True)
    )
    mix_back = line_gather(d_hidden.astype(bf16), "tensor")
    ffn_out = line_scatter(jnp.dot(inner_low, down_full, preferred_element_type=f32), "tensor")
    block_out = (local_mask * (hidden + ffn_out)).astype(bf16)
    grad_gate = contract(ffn_rows, d_gate, 0, 0).astype(bf16)
    grad_up = contract(ffn_rows, d_up, 0, 0).astype(bf16)
    grad_down = contract(inner_low, back_rows, 0, 0).astype(bf16)

    d_gated = contract(mix_back, out_full, 1, 1)
    d_proj, d_taps, d_par, d_gain = mixer_backward(
        slot_lengths, proj, taps, par, gain_row, d_gated, o, inv, new, state,
        heads_here, key_width, value_width,
    )
    grad_out = contract(gated, mix_back, 0, 0).astype(bf16)
    mixer_part = contract(d_proj, mix_full, 1, 1)
    grad_attn_gain = jnp.sum(mixer_part * block_unit, axis=0)
    cut = 2 * key_channels + value_channels
    grad_mix = [
        contract(mixer_rows, d_proj[:, :cut], 0, 0).astype(bf16),
        contract(mixer_rows, d_proj[:, cut:], 0, 0).astype(bf16),
    ]
    d_mixer_in = line_scatter(mixer_part, "tensor")
    block_scale = rms_rows(block_rows)
    unit = block_rows * block_scale
    dn = d_mixer_in * attn_gain
    grad_in = d_hidden + block_scale * (dn - unit * jnp.mean(dn * unit, axis=-1, keepdims=True))

    def owners(grad_piece, dim):
        return lax.psum_scatter(grad_piece, "dp", scatter_dimension=dim, tiled=True).astype(f32)

    sum_gate, sum_up, sum_down = owners(grad_gate, 0), owners(grad_up, 0), owners(grad_down, 1)
    sum_out = owners(grad_out, 1)
    sum_low, sum_high = owners(grad_mix[0], 0), owners(grad_mix[1], 0)

    shared = jnp.concatenate([grad_attn_gain, grad_ffn_gain, d_gain[0]])
    packed = jnp.concatenate([d_taps.reshape(-1), d_par[:2].reshape(-1), shared])
    width = packed.shape[0]
    padded = -(-width // 1024) * 1024
    packed = jnp.pad(packed, (0, padded - width)).reshape(padded // LANES, LANES)
    table = line_gather(cube_sum(packed, "dp"), "tensor").reshape(tensor_size, padded)
    taps_all = table[:, : d_taps.size].reshape((tensor_size,) + d_taps.shape)
    cuts = (0, key_channels, 2 * key_channels, 2 * key_channels + value_channels)
    conv_grad = jnp.concatenate(
        [
            taps_all[:, :, lo:hi].transpose(1, 0, 2).reshape(d_taps.shape[0], -1)
            for lo, hi in zip(cuts[:-1], cuts[1:])
        ],
        axis=1,
    )
    at = d_taps.size
    rate_grad = table[:, at : at + heads_here].reshape(-1)
    at += LANES
    bias_grad = table[:, at : at + heads_here].reshape(-1)
    at += LANES
    totals = jnp.sum(table[:, at : at + shared.shape[0]], axis=0)
    model = attn_gain.shape[0]
    gate_from = value_channels
    return (
        block_out,
        grad_in,
        totals[:model],
        sum_low[:, :key_channels],
        sum_low[:, key_channels : 2 * key_channels],
        sum_low[:, 2 * key_channels :],
        sum_high[:, :gate_from],
        sum_high[:, gate_from : gate_from + heads_here],
        sum_high[:, gate_from + heads_here : gate_from + 2 * heads_here],
        conv_grad,
        rate_grad,
        bias_grad,
        totals[2 * model :],
        sum_out,
        totals[model : 2 * model],
        sum_gate,
        sum_up,
        sum_down,
    )


def solution(mesh):
    rows = P(("dp", "tensor"), None)
    wide = P("dp", "tensor")
    tall = P("tensor", "dp")
    return jax.shard_map(
        body,
        mesh=mesh,
        in_specs=(
            rows, P("dp"), P(), wide, wide, wide, wide, wide, wide,
            P(), P(), P(), P(), tall, P(), wide, wide, tall, rows,
        ),
        out_specs=(
            rows, rows, P(), wide, wide, wide, wide, wide, wide,
            P(), P(), P(), P(), tall, P(), wide, wide, tall,
        ),
        check_vma=False,
    )
```

```python
import functools

import jax
import jax.numpy as jnp
from jax import lax
from jax.experimental import pallas as pl
from jax.experimental.pallas import tpu as pltpu
from jax.sharding import PartitionSpec as P

f32, bf16 = jnp.float32, jnp.bfloat16
HALO = 8
LANES = 128


def contract(left_in, right_in, left_dim, right_dim):
    return lax.dot_general(
        left_in, right_in, (((left_dim,), (right_dim,)), ((), ())), preferred_element_type=f32
    )


def dot_low(left_in, right_in, left_dim, right_dim):
    return contract(left_in.astype(bf16), right_in.astype(bf16), left_dim, right_dim)


def two_terms(value_in):
    high = value_in.astype(bf16)
    return high, (value_in - high.astype(f32)).astype(bf16)


def dot_split(left_in, right_in, left_dim, right_dim):
    (lh, ll), (rh, rl) = left_in, right_in
    return (
        contract(lh, rh, left_dim, right_dim)
        + contract(lh, rl, left_dim, right_dim)
        + contract(ll, rh, left_dim, right_dim)
    )


def sigmoid(value_in):
    return 1.0 / (1.0 + jnp.exp(-value_in))


def block_inverse(terms, base):
    size = terms[0].shape[0]
    rows = lax.broadcasted_iota(jnp.int32, (size, size), 0)
    cols = lax.broadcasted_iota(jnp.int32, (size, size), 1)
    eye = (rows == cols).astype(f32)
    near = (rows // base) == (cols // base)
    diag = [jnp.where(near, a, 0.0) for a in terms]
    off = [jnp.where(near, 0.0, a) for a in terms]
    power = diag
    inv = [eye - a for a in diag]
    for _ in range(base.bit_length() - 2):
        power = [dot_low(p, p, 1, 0) for p in power]
        inv = [x + dot_low(x, p, 1, 0) for x, p in zip(inv, power)]
    if size == base:
        return inv
    step = [dot_low(x, e, 1, 0) for x, e in zip(inv, off)]
    outer = [eye - n for n in step]
    power = step
    for _ in range((size // base).bit_length() - 2):
        power = [dot_low(p, p, 1, 0) for p in power]
        outer = [y + dot_low(y, p, 1, 0) for y, p in zip(outer, power)]
    return [dot_low(y, x, 1, 0) for y, x in zip(outer, inv)]


def small_terms(small, rate_row, bias_row, mask_col, heads, size):
    z = small + bias_row
    soft = jnp.maximum(z, 0.0) + jnp.log(1.0 + jnp.exp(-jnp.abs(z)))
    decay = -jnp.exp(rate_row) * soft
    rows = lax.broadcasted_iota(jnp.int32, (size, size), 0)
    cols = lax.broadcasted_iota(jnp.int32, (size, size), 1)
    tril = (rows >= cols).astype(bf16)
    hi, lo = two_terms(decay)
    lo2 = (decay - hi.astype(f32) - lo.astype(f32)).astype(bf16)
    cum = contract(tril, hi, 1, 0) + contract(tril, lo, 1, 0) + contract(tril, lo2, 1, 0)
    beta = sigmoid(small) * mask_col
    return z, decay, cum, beta


def conv_rows(ext_ref, taps_ref, size):
    total = None
    count = taps_ref.shape[0]
    for j in range(count):
        term = ext_ref[pl.ds(HALO - count + 1 + j, size), :] * taps_ref[pl.ds(j, 1), :]
        total = term if total is None else total + term
    return total


def unit_rows(pre, scale):
    sig = sigmoid(pre)
    y = pre * sig
    r = lax.rsqrt(jnp.sum(y * y, axis=-1, keepdims=True) + 1e-06)
    return sig, r, y * r


def mixer_forward_kernel(
    heads, kw, vw, size, base,
    len_ref, at_ref, proj_ref, halo_ref, taps_ref, par_ref, gain_ref,
    gated_ref, o_ref, x_ref, new_ref, s_ref,
    ext_ref, pre_ref, state_ref,
):
    slot, blk = pl.program_id(0), pl.program_id(1)
    conv_width = heads * (2 * kw + vw)
    small_at = conv_width

    @pl.when(blk == 0)
    def _():
        state_ref[...] = jnp.zeros_like(state_ref)

    ext_ref[pl.ds(0, HALO), :] = jnp.where(blk > 0, halo_ref[...], 0.0)
    ext_ref[pl.ds(HALO, size), :] = proj_ref[:, :conv_width]
    pre_ref[...] = conv_rows(ext_ref, taps_ref, size)
    pos = blk * size + lax.broadcasted_iota(jnp.int32, (size, 1), 0)
    mask_col = (pos < len_ref[slot]).astype(f32)
    small = proj_ref[:, small_at : small_at + 128]
    _, _, cum, beta = small_terms(small, par_ref[0:1, :], par_ref[1:2, :], mask_col, heads, size)
    cum_t = cum.T
    rows = lax.broadcasted_iota(jnp.int32, (size, size), 0)
    cols = lax.broadcasted_iota(jnp.int32, (size, size), 1)
    hs = range(heads)
    scale = kw ** (-0.5)
    q, k, v = [], [], []
    for h in hs:
        _, _, u = unit_rows(pre_ref[:, h * kw : (h + 1) * kw], 1.0)
        q.append((u * scale).astype(bf16))
        _, _, u = unit_rows(pre_ref[:, (heads + h) * kw : (heads + h + 1) * kw], 1.0)
        k.append(u)
        pv = pre_ref[:, 2 * heads * kw + h * vw : 2 * heads * kw + (h + 1) * vw]
        v.append(pv * sigmoid(pv))
    kl = [a.astype(bf16) for a in k]
    cc = [cum[:, h : h + 1] for h in hs]
    cr = [cum_t[h : h + 1, :] for h in hs]
    bc = [beta[:, heads + h : heads + h + 1] for h in hs]
    dec = [jnp.where(rows >= cols, jnp.exp(jnp.minimum(cc[h] - cr[h], 0.0)), 0.0) for h in hs]
    kk = [contract(kl[h], kl[h], 1, 1) for h in hs]
    qk = [contract(q[h], kl[h], 1, 1) for h in hs]
    a = [jnp.where(rows > cols, bc[h] * kk[h] * dec[h], 0.0) for h in hs]
    inv = block_inverse(a, base)
    sl = [state_ref[h].astype(bf16) for h in hs]
    ks = [contract(kl[h], sl[h], 1, 0) for h in hs]
    qs = [contract(q[h], sl[h], 1, 0) for h in hs]
    ec = [jnp.exp(cc[h]) for h in hs]
    rhs = [bc[h] * (v[h] - ec[h] * ks[h]) for h in hs]
    new = [dot_split(two_terms(inv[h]), two_terms(rhs[h]), 1, 0) for h in hs]
    new2 = [two_terms(new[h]) for h in hs]
    o = [ec[h] * qs[h] + dot_split(two_terms(qk[h] * dec[h]), new2[h], 1, 0) for h in hs]
    for h in hs:
        s_ref[0, h] = state_ref[h]
        last = cum[size - 1 : size, h : h + 1]
        kel = (k[h] * jnp.exp(last - cc[h])).astype(bf16)
        state_ref[h] = jnp.exp(last) * state_ref[h] + contract(kel, new2[h][0], 0, 0)
        x_ref[:, h * size : (h + 1) * size] = inv[h]
        new_ref[:, h * vw : (h + 1) * vw] = new[h]
        o_ref[:, h * vw : (h + 1) * vw] = o[h]
        r = lax.rsqrt(jnp.mean(o[h] * o[h], axis=-1, keepdims=True) + 1e-05)
        g = proj_ref[:, small_at + LANES + h * vw : small_at + LANES + (h + 1) * vw]
        gated_ref[:, h * vw : (h + 1) * vw] = (
            o[h] * r * gain_ref[...] * (g * sigmoid(g))
        ).astype(bf16)


def mixer_backward_kernel(
    heads, kw, vw, size, base,
    len_ref, at_ref, proj_ref, halo_ref, taps_ref, par_ref, do_ref, dhead_ref, x_ref, new_ref, s_ref,
    dproj_ref, dmix_ref, dtaps_ref, dpar_ref,
    ext_ref, pre_ref, dext_ref, dstate_ref,
):
    slot, step = pl.program_id(0), pl.program_id(1)
    blk = pl.num_programs(1) - 1 - step
    conv_width = heads * (2 * kw + vw)
    small_at = conv_width
    count = taps_ref.shape[0]

    @pl.when((step == 0) & (slot == 0))
    def _():
        dtaps_ref[...] = jnp.zeros_like(dtaps_ref)
        dpar_ref[...] = jnp.zeros_like(dpar_ref)

    @pl.when(step == 0)
    def _():
        dstate_ref[...] = jnp.zeros_like(dstate_ref)
        dext_ref[pl.ds(0, HALO), :] = jnp.zeros((HALO, conv_width), f32)

    dext_ref[pl.ds(size, HALO), :] = dext_ref[pl.ds(0, HALO), :]
    ext_ref[pl.ds(0, HALO), :] = jnp.where(blk > 0, halo_ref[...], 0.0)
    ext_ref[pl.ds(HALO, size), :] = proj_ref[:, :conv_width]
    pre_ref[...] = conv_rows(ext_ref, taps_ref, size)
    pos = blk * size + lax.broadcasted_iota(jnp.int32, (size, 1), 0)
    mask_col = (pos < len_ref[slot]).astype(f32)
    small = proj_ref[:, small_at : small_at + 128]
    z, decay, cum, beta = small_terms(small, par_ref[0:1, :], par_ref[1:2, :], mask_col, heads, size)
    cum_t = cum.T
    rows = lax.broadcasted_iota(jnp.int32, (size, size), 0)
    cols = lax.broadcasted_iota(jnp.int32, (size, size), 1)
    hs = range(heads)
    scale = kw ** (-0.5)
    at_q = [slice(h * kw, (h + 1) * kw) for h in hs]
    at_k = [slice((heads + h) * kw, (heads + h + 1) * kw) for h in hs]
    at_v = [slice(2 * heads * kw + h * vw, 2 * heads * kw + (h + 1) * vw) for h in hs]
    at_o = [slice(h * vw, (h + 1) * vw) for h in hs]
    cc = [cum[:, h : h + 1] for h in hs]
    cr = [cum_t[h : h + 1, :] for h in hs]
    bc = [beta[:, heads + h : heads + h + 1] for h in hs]
    ec = [jnp.exp(cc[h]) for h in hs]
    do = [do_ref[:, at_o[h]] for h in hs]
    q, k, ql, kl = [], [], [], []
    for h in hs:
        _, _, u = unit_rows(pre_ref[:, at_q[h]], 1.0)
        q.append(u * scale)
        _, _, u = unit_rows(pre_ref[:, at_k[h]], 1.0)
        k.append(u)
    ql = [u.astype(bf16) for u in q]
    kl = [u.astype(bf16) for u in k]
    dec = [jnp.where(rows >= cols, jnp.exp(jnp.minimum(cc[h] - cr[h], 0.0)), 0.0) for h in hs]
    kk = [contract(kl[h], kl[h], 1, 1) for h in hs]
    qk = [contract(ql[h], kl[h], 1, 1) for h in hs]
    pm = [qk[h] * dec[h] for h in hs]
    sl = [s_ref[0, h].astype(bf16) for h in hs]
    tl = [dstate_ref[h].astype(bf16) for h in hs]
    ks = [contract(kl[h], sl[h], 1, 0) for h in hs]
    qs = [contract(ql[h], sl[h], 1, 0) for h in hs]
    new2 = [two_terms(new_ref[:, at_o[h]]) for h in hs]
    do2 = [two_terms(do[h]) for h in hs]
    last = [cum[size - 1 : size, h : h + 1] for h in hs]
    el = [jnp.exp(last[h] - cc[h]) for h in hs]
    kel = [(k[h] * el[h]).astype(bf16) for h in hs]
    dpm = [dot_split(do2[h], new2[h], 1, 1) for h in hs]
    dnew = [dot_split(two_terms(pm[h]), do2[h], 0, 0) + contract(kel[h], tl[h], 1, 0) for h in hs]
    drhs = [dot_split(two_terms(x_ref[:, h * size : (h + 1) * size]), two_terms(dnew[h]), 0, 0) for h in hs]
    da = [-dot_split(two_terms(drhs[h]), new2[h], 1, 1) for h in hs]
    dkel = [contract(new2[h][0], tl[h], 1, 1) for h in hs]
    dcol, dbeta = [], []
    dq, dk, edo, edz = [], [], [], []
    lastrow = (lax.broadcasted_iota(jnp.int32, (size, 1), 0) == size - 1).astype(f32)
    for h in hs:
        pv = pre_ref[:, at_v[h]]
        sv = sigmoid(pv)
        zz = pv * sv - ec[h] * ks[h]
        dz = bc[h] * drhs[h]
        db = jnp.sum(drhs[h] * zz, axis=-1, keepdims=True)
        dext_ref[pl.ds(0, size), at_v[h]] = dz * (sv * (1.0 + pv * (1.0 - sv)))
        edo.append((ec[h] * do[h]).astype(bf16))
        edz.append((-ec[h] * dz).astype(bf16))
        dec_col = jnp.sum(do[h] * qs[h] - dz * ks[h], axis=-1, keepdims=True)
        dam = jnp.where(rows > cols, da[h], 0.0)
        dpmm = jnp.where(rows >= cols, dpm[h], 0.0)
        kd = kk[h] * dec[h]
        db = db + jnp.sum(dam * kd, axis=-1, keepdims=True)
        dspread = dpmm * pm[h] + dam * (bc[h] * kd)
        dqk = (dpmm * dec[h]).astype(bf16)
        dkk = (dam * (bc[h] * dec[h])).astype(bf16)
        d_el = jnp.sum(dkel[h] * k[h], axis=-1, keepdims=True) * el[h]
        d_keep = jnp.sum(jnp.sum(dstate_ref[h] * s_ref[0, h], axis=-1, keepdims=True), axis=0, keepdims=True)
        d_last = d_keep * jnp.exp(last[h]) + jnp.sum(d_el, axis=0, keepdims=True)
        col = jnp.sum(dspread, axis=-1, keepdims=True) + dec_col * ec[h] - d_el + lastrow * d_last
        row = jnp.sum(dspread, axis=0, keepdims=True)
        dcol.append((col, row))
        dbeta.append(db)
        dq.append(contract(edo[h], sl[h], 1, 1) + contract(dqk, kl[h], 1, 0))
        dk.append(
            contract(edz[h], sl[h], 1, 1)
            + dkel[h] * el[h]
            + contract(dqk, ql[h], 0, 0)
            + contract(dkk, kl[h], 1, 0)
            + contract(dkk, kl[h], 0, 0)
        )
    for h in hs:
        dstate_ref[h] = (
            jnp.exp(last[h]) * dstate_ref[h]
            + contract(ql[h], edo[h], 0, 0)
            + contract(kl[h], edz[h], 0, 0)
        )
        for at, grad, fac in ((at_q[h], dq[h], scale), (at_k[h], dk[h], 1.0)):
            pre = pre_ref[:, at]
            sig, r, u = unit_rows(pre, 1.0)
            du = grad * fac
            dy = r * (du - u * jnp.sum(u * du, axis=-1, keepdims=True))
            dext_ref[pl.ds(0, size), at] = dy * (sig * (1.0 + pre * (1.0 - sig)))
    lanes = lax.broadcasted_iota(jnp.int32, (size, 128), 1)
    subs = lax.broadcasted_iota(jnp.int32, (128, size), 0)
    dcum = jnp.zeros((size, 128), f32)
    drow = jnp.zeros((128, size), f32)
    dbeta_all = jnp.zeros((size, 128), f32)
    for h in hs:
        dcum = jnp.where(lanes == h, dcol[h][0], dcum)
        drow = jnp.where(subs == h, dcol[h][1], drow)
        dbeta_all = jnp.where(lanes == heads + h, dbeta[h], dbeta_all)
    dcum = dcum - drow.T
    triu = (rows <= cols).astype(bf16)
    hi, lo = two_terms(dcum)
    ddecay = contract(triu, hi, 1, 0) + contract(triu, lo, 1, 0)
    dz = ddecay * (-jnp.exp(par_ref[0:1, :])) * sigmoid(z)
    dpar_ref[0:1, :] += jnp.sum(ddecay * decay, axis=0, keepdims=True)
    dpar_ref[1:2, :] += jnp.sum(dz, axis=0, keepdims=True)
    sb = sigmoid(small)
    dsmall = dz + dbeta_all * mask_col * sb * (1.0 - sb)
    dproj_ref[:, small_at : small_at + LANES] = dsmall.astype(bf16)
    dmix_ref[:, small_at : small_at + LANES] = dsmall.astype(bf16)
    dproj_ref[:, small_at + LANES :] = dhead_ref[...]
    dpre = dext_ref[pl.ds(0, size), :]
    total = None
    for j in range(count):
        back = dext_ref[pl.ds(count - 1 - j, size), :] * taps_ref[pl.ds(j, 1), :]
        total = back if total is None else total + back
        seen = ext_ref[pl.ds(HALO - count + 1 + j, size), :]
        dtaps_ref[pl.ds(j, 1), :] += jnp.sum(dpre * seen, axis=0, keepdims=True)
    dproj_ref[:, :conv_width] = total.astype(bf16)
    dmix_ref[:, :conv_width] = total.astype(bf16)


def mixer_specs(heads, kw, vw, size, blocks, width, taps, per_owner, order):
    conv_width = heads * (2 * kw + vw)
    per = size // HALO

    def place(index, at_ref):
        return at_ref[index // per_owner] * per_owner + lax.rem(index, per_owner)

    def at(s, b, len_ref, at_ref):
        return place(s * blocks + order(b), at_ref), 0

    def before(s, b, len_ref, at_ref):
        index = jnp.maximum(s * blocks + order(b) - 1, 0)
        return place(index, at_ref) * per + per - 1, 0

    return dict(
        proj=pl.BlockSpec((size, width), at),
        mix=pl.BlockSpec((size, conv_width + LANES), at),
        halo=pl.BlockSpec((HALO, conv_width), before),
        taps=pl.BlockSpec((taps, conv_width), lambda s, b, *_: (0, 0)),
        par=pl.BlockSpec((8, LANES), lambda s, b, *_: (0, 0)),
        gain=pl.BlockSpec((1, vw), lambda s, b, *_: (0, 0)),
        value=pl.BlockSpec((size, heads * vw), at),
        inv=pl.BlockSpec((size, heads * size), at),
        state=pl.BlockSpec((1, heads, kw, vw), lambda s, b, *_: (s * blocks + order(b), 0, 0, 0)),
    )


def mixer_forward(lengths, place, proj, taps, par, gain, heads, kw, vw, size=128, base=16):
    slots = lengths.shape[0]
    rows, width = proj.shape
    blocks = rows // slots // size
    per_owner = rows // size // place.shape[0]
    sp = mixer_specs(
        heads, kw, vw, size, blocks, width, taps.shape[0], per_owner, lambda b: b
    )
    conv_width = heads * (2 * kw + vw)
    return pl.pallas_call(
        functools.partial(mixer_forward_kernel, heads, kw, vw, size, base),
        grid_spec=pltpu.PrefetchScalarGridSpec(
            num_scalar_prefetch=2,
            grid=(slots, blocks),
            in_specs=[sp[n] for n in ("proj", "halo", "taps", "par", "gain")],
            out_specs=[sp[n] for n in ("value", "value", "inv", "value", "state")],
            scratch_shapes=[
                pltpu.VMEM((size + HALO, conv_width), f32),
                pltpu.VMEM((size, conv_width), f32),
                pltpu.VMEM((heads, kw, vw), f32),
            ],
        ),
        out_shape=[
            jax.ShapeDtypeStruct((rows, heads * vw), bf16),
            jax.ShapeDtypeStruct((rows, heads * vw), f32),
            jax.ShapeDtypeStruct((rows, heads * size), f32),
            jax.ShapeDtypeStruct((rows, heads * vw), f32),
            jax.ShapeDtypeStruct((slots * blocks, heads, kw, vw), f32),
        ],
        compiler_params=pltpu.CompilerParams(dimension_semantics=("arbitrary", "arbitrary")),
        cost_estimate=pl.CostEstimate(
            flops=rows * heads * 8000000, bytes_accessed=rows * width * 12, transcendentals=rows * width
        ),
        name="mixer_forward",
    )(lengths, place, proj, proj, taps, par, gain)


def mixer_backward(
    lengths, place, proj, taps, par, d_out, d_head, inv, new, state, heads, kw, vw, size=128, base=16
):
    slots = lengths.shape[0]
    rows, width = proj.shape
    blocks = rows // slots // size
    per_owner = rows // size // place.shape[0]
    sp = mixer_specs(
        heads, kw, vw, size, blocks, width, taps.shape[0], per_owner, lambda b: blocks - 1 - b
    )
    conv_width = heads * (2 * kw + vw)
    return pl.pallas_call(
        functools.partial(mixer_backward_kernel, heads, kw, vw, size, base),
        grid_spec=pltpu.PrefetchScalarGridSpec(
            num_scalar_prefetch=2,
            grid=(slots, blocks),
            in_specs=[
                sp[n]
                for n in ("mix", "halo", "taps", "par", "value", "value", "inv", "value", "state")
            ],
            out_specs=[sp[n] for n in ("proj", "mix", "taps", "par")],
            scratch_shapes=[
                pltpu.VMEM((size + HALO, conv_width), f32),
                pltpu.VMEM((size, conv_width), f32),
                pltpu.VMEM((size + HALO, conv_width), f32),
                pltpu.VMEM((heads, kw, vw), f32),
            ],
        ),
        out_shape=[
            jax.ShapeDtypeStruct((rows, width), bf16),
            jax.ShapeDtypeStruct((rows, conv_width + LANES), bf16),
            jax.ShapeDtypeStruct(taps.shape, f32),
            jax.ShapeDtypeStruct((8, LANES), f32),
        ],
        compiler_params=pltpu.CompilerParams(dimension_semantics=("arbitrary", "arbitrary")),
        cost_estimate=pl.CostEstimate(
            flops=rows * heads * 12000000, bytes_accessed=rows * width * 12, transcendentals=rows * width
        ),
        name="mixer_backward",
    )(lengths, place, proj, proj, taps, par, d_out, d_head, inv, new, state)


def head_backward_kernel(heads, vw, gain_ref, d_ref, o_ref, head_ref, dout_ref, dhead_ref, dgain_ref):
    @pl.when(pl.program_id(0) == 0)
    def _():
        dgain_ref[...] = jnp.zeros_like(dgain_ref)

    gain = gain_ref[...]
    total = jnp.zeros_like(gain)
    for h in range(heads):
        at = slice(h * vw, (h + 1) * vw)
        g = head_ref[:, at]
        sig = sigmoid(g)
        silu = g * sig
        o = o_ref[:, at]
        r = lax.rsqrt(jnp.mean(o * o, axis=-1, keepdims=True) + 1e-05)
        unit = o * r
        d = d_ref[:, at]
        both = d * unit
        dhead_ref[:, at] = (both * gain * (sig * (1.0 + g * (1.0 - sig)))).astype(bf16)
        total = total + jnp.sum(both * silu, axis=0, keepdims=True)
        dn = d * gain * silu
        dout_ref[:, at] = r * (dn - unit * jnp.mean(unit * dn, axis=-1, keepdims=True))
    dgain_ref[...] += total


def head_backward(gain, d_gated, o, proj, heads, vw, size=256):
    rows, width = o.shape
    size = min(size, rows)
    block = pl.BlockSpec((size, width), lambda i: (i, 0))
    row = pl.BlockSpec((1, vw), lambda i: (0, 0))
    start = proj.shape[1] - width
    cols = pl.BlockSpec((pl.Element(size), pl.Element(width)), lambda i: (i * size, start))
    return pl.pallas_call(
        functools.partial(head_backward_kernel, heads, vw),
        grid=(rows // size,),
        in_specs=[row, block, block, cols],
        out_specs=[block, block, row],
        out_shape=[
            jax.ShapeDtypeStruct((rows, width), f32),
            jax.ShapeDtypeStruct((rows, width), bf16),
            jax.ShapeDtypeStruct((1, vw), f32),
        ],
        cost_estimate=pl.CostEstimate(
            flops=rows * width * 30, bytes_accessed=rows * width * 18, transcendentals=rows * width
        ),
        name="head_backward",
    )(gain, d_gated, o, proj)


def turn(value_in):
    size = lax.axis_size("tensor")
    return lax.ppermute(value_in, "tensor", [(i, (i + 1) % size) for i in range(size)])


def after(value_in, *others):
    return lax.optimization_barrier((value_in,) + others)[0]


def ring_gather(piece):
    pieces = [piece]
    for _ in range(lax.axis_size("tensor") - 1):
        pieces.append(turn(pieces[-1]))
    return pieces[1:] + pieces[:1]


def ring_scatter(pieces):
    total = None
    for piece in pieces[:-1]:
        send = piece.astype(f32)
        if total is not None:
            send = send + total.astype(f32)
        total = turn(send.astype(bf16))
    return pieces[-1].astype(f32) + total.astype(f32)


def cube_bits():
    me = lax.axis_index("dp")
    return lax.rem(me, 2), lax.rem(me // 2, 2), me // 4


def cube_halves(array, bit, dim):
    mine = cube_bits()[bit]
    keep = lax.dynamic_index_in_dim(array, mine, dim, keepdims=False)
    send = lax.dynamic_index_in_dim(array, 1 - mine, dim, keepdims=False)
    pairs = [(i, i ^ (1 << bit)) for i in range(lax.axis_size("dp"))]
    return keep, lax.ppermute(send, "dp", pairs)


def joined(pair):
    return (pair[0].astype(f32) + pair[1].astype(f32)).astype(bf16)


def cube_first(value_in):
    if lax.axis_size("dp") != 8:
        return (value_in,)
    return cube_halves(value_in.reshape(2, 2, 2, value_in.shape[0] // 8, -1), 0, 2)


def cube_second(held):
    if len(held) == 1:
        return held
    whole = joined(held)
    half = whole.shape[2] // 2
    return cube_halves(whole[:, :, :half], 1, 1) + cube_halves(whole[:, :, half:], 2, 0)


def cube_third(held):
    if len(held) == 1:
        return held
    return cube_halves(joined(held[:2]), 2, 0) + cube_halves(joined(held[2:]), 1, 0)


def cube_columns(held, lo, hi):
    if len(held) == 1:
        return lax.psum_scatter(held[0][:, lo:hi], "dp", scatter_dimension=0, tiled=True).astype(f32)
    cut = [piece[:, lo:hi].astype(f32) for piece in held]
    return jnp.concatenate([cut[0] + cut[1], cut[2] + cut[3]])


def meet(*values):
    return lax.optimization_barrier(values)


def cube_sum(value_in, axis):
    size = lax.axis_size(axis)
    if size & (size - 1):
        return lax.psum(value_in, axis)
    bit = 1
    while bit < size:
        value_in = value_in + lax.ppermute(value_in, axis, [(i, i ^ bit) for i in range(size)])
        bit *= 2
    return value_in


def rms_rows(value_in):
    return lax.rsqrt(jnp.mean(value_in * value_in, axis=-1, keepdims=True) + 1e-05)


def body(
    block_in,
    slot_lengths,
    attn_gain,
    query_weight,
    key_weight,
    value_weight,
    output_gate,
    decay_weight,
    beta_weight,
    conv_weight,
    decay_log,
    step_bias,
    head_gain,
    out_weight,
    ffn_gain,
    gate_weight,
    up_weight,
    down_weight,
    out_grad,
):
    tensor_size = lax.axis_size("tensor")
    tensor_rank = lax.axis_index("tensor")
    local_rows = block_in.shape[0]
    group_rows = local_rows * tensor_size
    slots_here = slot_lengths.shape[0]
    slot_length = group_rows // slots_here
    heads_here = decay_weight.shape[1]
    total_heads = decay_log.shape[0]
    key_channels = query_weight.shape[1]
    value_channels = value_weight.shape[1]
    key_width = key_channels // heads_here
    value_width = value_channels // heads_here
    model = attn_gain.shape[0]
    ring = range(tensor_size)
    row_of = tensor_rank * local_rows + jnp.arange(local_rows, dtype=jnp.int32)
    local_mask = (
        lax.rem(row_of, slot_length) < jnp.take(slot_lengths, row_of // slot_length)
    ).astype(f32)[:, None]
    place = lax.rem(
        tensor_rank - jnp.arange(tensor_size, dtype=jnp.int32) + 2 * tensor_size - 1, tensor_size
    )
    query_start = tensor_rank * key_channels
    key_start = total_heads * key_width + tensor_rank * key_channels
    value_start = 2 * total_heads * key_width + tensor_rank * value_channels
    taps = jnp.concatenate(
        [
            lax.dynamic_slice_in_dim(conv_weight, query_start, key_channels, 1),
            lax.dynamic_slice_in_dim(conv_weight, key_start, key_channels, 1),
            lax.dynamic_slice_in_dim(conv_weight, value_start, value_channels, 1),
        ],
        axis=1,
    )
    rate_local = lax.dynamic_slice_in_dim(decay_log, tensor_rank * heads_here, heads_here)
    bias_local = lax.dynamic_slice_in_dim(step_bias, tensor_rank * heads_here, heads_here)
    par = jnp.pad(jnp.stack([rate_local, bias_local]), ((0, 6), (0, LANES - heads_here)))

    small_local = jnp.concatenate([decay_weight, beta_weight], axis=1)
    mix_local = jnp.concatenate(
        [
            query_weight,
            key_weight,
            value_weight,
            jnp.pad(small_local, ((0, 0), (0, LANES - 2 * heads_here))),
            output_gate,
        ],
        axis=1,
    )
    mix_full = lax.all_gather(mix_local, "dp", axis=0, tiled=True)
    block_pieces = ring_gather(block_in)
    out_full = lax.all_gather(out_weight, "dp", axis=1, tiled=True)
    gate_full = lax.all_gather(gate_weight, "dp", axis=0, tiled=True)
    up_full = lax.all_gather(up_weight, "dp", axis=0, tiled=True)
    down_full = lax.all_gather(down_weight, "dp", axis=1, tiled=True)

    def owners(grad_piece, dim):
        return lax.psum_scatter(grad_piece, "dp", scatter_dimension=dim, tiled=True).astype(f32)

    units, mixer_pieces = [], []
    for piece in block_pieces:
        piece = piece.astype(f32)
        units.append(piece * rms_rows(piece))
        mixer_pieces.append((units[-1] * attn_gain).astype(bf16))
    out_masked = out_grad.astype(f32) * local_mask
    mixer_rows = jnp.concatenate(mixer_pieces)
    proj = jnp.dot(mixer_rows, mix_full, preferred_element_type=f32)
    back_own = after(out_masked.astype(bf16), block_pieces[-2])
    back_pieces = [turn(back_own)]
    proj = after(proj, back_pieces[0])
    back_pieces.append(turn(after(back_pieces[0], proj)))
    gated, o, inv, new, state = mixer_forward(
        slot_lengths, place, proj, taps, par, head_gain[None, :], heads_here, key_width, value_width
    )
    gated = after(gated, back_pieces[1])
    for _ in range(3, tensor_size):
        back_pieces.append(turn(back_pieces[-1]))
    back_pieces.append(back_own)

    def split(rows_in):
        return [rows_in[i * local_rows : (i + 1) * local_rows] for i in ring]

    mixer_out = ring_scatter(split(jnp.dot(gated, out_full, preferred_element_type=f32)))
    hidden = block_in.astype(f32) + mixer_out
    hidden_scale = rms_rows(hidden)
    hidden_unit = hidden * hidden_scale

    ffn_pieces = ring_gather((hidden_unit * ffn_gain).astype(bf16))
    inner_pieces, gate_pieces, up_pieces, part_pieces = [], [], [], []
    for piece, back in zip(ffn_pieces, back_pieces):
        gate_act = jnp.dot(piece, gate_full, preferred_element_type=f32)
        up_act = jnp.dot(piece, up_full, preferred_element_type=f32)
        gate_sig = jax.nn.sigmoid(gate_act)
        gate_silu = gate_act * gate_sig
        inner_pieces.append((gate_silu * up_act).astype(bf16))
        d_inner = contract(back, down_full, 1, 1)
        d_gate = (d_inner * up_act * gate_sig * (1.0 + gate_act * (1.0 - gate_sig))).astype(bf16)
        d_up = (d_inner * gate_silu).astype(bf16)
        gate_pieces.append(d_gate)
        up_pieces.append(d_up)
        part_pieces.append(contract(d_gate, gate_full, 1, 1) + contract(d_up, up_full, 1, 1))
    d_ffn_in = ring_scatter(part_pieces)
    grad_ffn_gain = jnp.sum(d_ffn_in * hidden_unit, axis=0)
    dn = d_ffn_in * ffn_gain
    d_hidden = out_masked + hidden_scale * (
        dn - hidden_unit * jnp.mean(dn * hidden_unit, axis=-1, keepdims=True)
    )
    mix_own = d_hidden.astype(bf16)
    ffn_rows = jnp.concatenate([after(p, mix_own) for p in ffn_pieces])
    inner_rows = jnp.concatenate([after(p, mix_own) for p in inner_pieces])

    hop, ffn_out_part, grad_gate = meet(
        turn(mix_own),
        jnp.dot(inner_rows, down_full, preferred_element_type=f32),
        contract(ffn_rows, jnp.concatenate(gate_pieces), 0, 0).astype(bf16),
    )
    mix_pieces = [hop]
    sum_gate = owners(grad_gate, 0)
    up_rows = jnp.concatenate([after(p, hop) for p in up_pieces])
    hop, grad_up, grad_down = meet(
        turn(hop),
        contract(ffn_rows, up_rows, 0, 0).astype(bf16),
        contract(after(inner_rows, hop), jnp.concatenate(back_pieces), 0, 0).astype(bf16),
    )
    mix_pieces.append(hop)
    sum_up, sum_down = owners(grad_up, 0), owners(grad_down, 1)
    out_pieces = split(ffn_out_part)
    out_total = turn(after(out_pieces[0].astype(bf16), hop))
    for _ in range(3, tensor_size):
        hop = turn(hop)
        mix_pieces.append(hop)
    mix_back, out_total = meet(jnp.concatenate(mix_pieces + [mix_own]), out_total)

    d_gated = contract(mix_back, out_full, 1, 1)
    d_out, d_head, grad_head_gain = head_backward(
        head_gain[None, :], d_gated, o, proj, heads_here, value_width
    )
    out_total = turn((after(out_pieces[1], mix_back) + out_total.astype(f32)).astype(bf16))
    grad_out = contract(gated, mix_back, 0, 0).astype(bf16)
    d_out = after(d_out, out_total, grad_out)
    for index in range(2, tensor_size - 1):
        out_total = turn((after(out_pieces[index], d_out) + out_total.astype(f32)).astype(bf16))
    d_proj, d_mix, d_taps, d_par = mixer_backward(
        slot_lengths, place, proj, taps, par, d_out, d_head, inv, new, state,
        heads_here, key_width, value_width,
    )
    cut = 2 * local_rows
    d_proj = after(d_proj, out_total)
    early = contract(d_proj[:cut], mix_full, 1, 1).astype(bf16)
    first, second = meet(early[:local_rows], early[local_rows:])
    sum_out = owners(after(grad_out, first), 1)
    total, grad_mix = meet(
        turn(first), contract(mixer_rows, after(d_mix, first), 0, 0).astype(bf16)
    )
    rest = contract(after(d_proj[cut:], total), mix_full, 1, 1).astype(bf16)
    total, held, rest = meet(
        turn((second.astype(f32) + total.astype(f32)).astype(bf16)), cube_first(grad_mix), rest
    )
    mixer_parts = [first, second] + [
        rest[i * local_rows : (i + 1) * local_rows] for i in range(tensor_size - 2)
    ]
    held = cube_second(held)
    grad_head = contract(mixer_rows, after(d_head, total), 0, 0).astype(bf16)
    sum_head = owners(grad_head, 0)
    grad_attn_gain = sum(
        jnp.sum(p.astype(f32) * u, axis=0) for p, u in zip(mixer_parts, units)
    )
    for index in range(2, tensor_size - 1):
        total = turn((mixer_parts[index].astype(f32) + total.astype(f32)).astype(bf16))
    total, held = meet(total, held)
    held = cube_third(held)
    d_mixer_in = mixer_parts[-1].astype(f32) + total.astype(f32)
    ffn_out = out_pieces[-1] + out_total.astype(f32)
    block_out = (local_mask * (hidden + ffn_out)).astype(bf16)
    block_scale = rms_rows(block_in.astype(f32))
    unit = units[-1]
    dn = d_mixer_in * attn_gain
    grad_in = d_hidden + block_scale * (dn - unit * jnp.mean(dn * unit, axis=-1, keepdims=True))

    shared = jnp.concatenate([grad_attn_gain, grad_ffn_gain, grad_head_gain[0]])
    packed = jnp.concatenate([d_taps.reshape(-1), d_par[:2].reshape(-1), shared])
    width = packed.shape[0]
    padded = -(-width // 1024) * 1024
    packed = jnp.pad(packed, (0, padded - width)).reshape(padded // LANES, LANES)
    table = jnp.stack(ring_gather(cube_sum(packed, "dp")))
    table = jnp.take(table, place, axis=0).reshape(tensor_size, padded)
    taps_all = table[:, : d_taps.size].reshape((tensor_size,) + d_taps.shape)
    cuts = (0, key_channels, 2 * key_channels, 2 * key_channels + value_channels)
    conv_grad = jnp.concatenate(
        [
            taps_all[:, :, lo:hi].transpose(1, 0, 2).reshape(d_taps.shape[0], -1)
            for lo, hi in zip(cuts[:-1], cuts[1:])
        ],
        axis=1,
    )
    at = d_taps.size
    rate_grad = table[:, at : at + heads_here].reshape(-1)
    at += LANES
    bias_grad = table[:, at : at + heads_here].reshape(-1)
    at += LANES
    totals = jnp.sum(table[:, at : at + shared.shape[0]], axis=0)
    sum_small = cube_columns(held, cuts[-1], cuts[-1] + LANES)
    return (
        block_out,
        grad_in,
        totals[:model],
        cube_columns(held, 0, cuts[1]),
        cube_columns(held, cuts[1], cuts[2]),
        cube_columns(held, cuts[2], cuts[3]),
        sum_head,
        sum_small[:, :heads_here],
        sum_small[:, heads_here : 2 * heads_here],
        conv_grad,
        rate_grad,
        bias_grad,
        totals[2 * model :],
        sum_out,
        totals[model : 2 * model],
        sum_gate,
        sum_up,
        sum_down,
    )


def solution(mesh):
    rows = P(("dp", "tensor"), None)
    wide = P("dp", "tensor")
    tall = P("tensor", "dp")
    return jax.shard_map(
        body,
        mesh=mesh,
        in_specs=(
            rows, P("dp"), P(), wide, wide, wide, wide, wide, wide,
            P(), P(), P(), P(), tall, P(), wide, wide, tall, rows,
        ),
        out_specs=(
            rows, rows, P(), wide, wide, wide, wide, wide, wide,
            P(), P(), P(), P(), tall, P(), wide, wide, tall,
        ),
        check_vma=False,
    )
```

```python
import functools

import jax
import jax.numpy as jnp
from jax import lax
from jax.experimental import pallas as pl
from jax.experimental.pallas import tpu as pltpu
from jax.sharding import PartitionSpec as P

f32, bf16 = jnp.float32, jnp.bfloat16
HALO = 8
LANES = 128


def contract(left_in, right_in, left_dim, right_dim):
    return lax.dot_general(
        left_in, right_in, (((left_dim,), (right_dim,)), ((), ())), preferred_element_type=f32
    )


def dot_low(left_in, right_in, left_dim, right_dim):
    return contract(left_in.astype(bf16), right_in.astype(bf16), left_dim, right_dim)


def two_terms(value_in):
    high = value_in.astype(bf16)
    return high, (value_in - high.astype(f32)).astype(bf16)


def dot_split(left_in, right_in, left_dim, right_dim):
    (lh, ll), (rh, rl) = left_in, right_in
    return (
        contract(lh, rh, left_dim, right_dim)
        + contract(lh, rl, left_dim, right_dim)
        + contract(ll, rh, left_dim, right_dim)
    )


def sigmoid(value_in):
    return 0.5 * jnp.tanh(0.5 * value_in) + 0.5


def block_inverse(terms, base):
    size = terms[0].shape[0]
    rows = lax.broadcasted_iota(jnp.int32, (size, size), 0)
    cols = lax.broadcasted_iota(jnp.int32, (size, size), 1)
    eye = (rows == cols).astype(f32)
    near = (rows // base) == (cols // base)
    diag = [jnp.where(near, a, 0.0) for a in terms]
    off = [jnp.where(near, 0.0, a) for a in terms]
    power = diag
    inv = [eye - a for a in diag]
    for _ in range(base.bit_length() - 2):
        power = [dot_low(p, p, 1, 0) for p in power]
        inv = [x + dot_low(x, p, 1, 0) for x, p in zip(inv, power)]
    if size == base:
        return inv
    step = [dot_low(x, e, 1, 0) for x, e in zip(inv, off)]
    outer = [eye - n for n in step]
    power = step
    for _ in range((size // base).bit_length() - 2):
        power = [dot_low(p, p, 1, 0) for p in power]
        outer = [y + dot_low(y, p, 1, 0) for y, p in zip(outer, power)]
    return [dot_low(y, x, 1, 0) for y, x in zip(outer, inv)]


def small_terms(small, rate_row, bias_row, mask_col, heads, size):
    z = small + bias_row
    soft = jnp.maximum(z, 0.0) + jnp.log(1.0 + jnp.exp(-jnp.abs(z)))
    decay = -jnp.exp(rate_row) * soft
    rows = lax.broadcasted_iota(jnp.int32, (size, size), 0)
    cols = lax.broadcasted_iota(jnp.int32, (size, size), 1)
    tril = (rows >= cols).astype(bf16)
    hi, lo = two_terms(decay)
    lo2 = (decay - hi.astype(f32) - lo.astype(f32)).astype(bf16)
    cum = contract(tril, hi, 1, 0) + contract(tril, lo, 1, 0) + contract(tril, lo2, 1, 0)
    beta = sigmoid(small) * mask_col
    return z, decay, cum, beta


def conv_rows(ext_ref, taps_ref, size):
    total = None
    count = taps_ref.shape[0]
    for j in range(count):
        term = ext_ref[pl.ds(HALO - count + 1 + j, size), :] * taps_ref[pl.ds(j, 1), :]
        total = term if total is None else total + term
    return total


def unit_rows(pre, scale):
    sig = sigmoid(pre)
    y = pre * sig
    r = lax.rsqrt(jnp.sum(y * y, axis=-1, keepdims=True) + 1e-06)
    return sig, r, y * r


def mixer_forward_kernel(
    heads, kw, vw, size, base,
    len_ref, at_ref, proj_ref, halo_ref, taps_ref, par_ref, gain_ref,
    gated_ref, o_ref, x_ref, new_ref, s_ref,
    ext_ref, pre_ref, state_ref,
):
    slot, blk = pl.program_id(0), pl.program_id(1)
    conv_width = heads * (2 * kw + vw)
    small_at = conv_width

    @pl.when(blk == 0)
    def _():
        state_ref[...] = jnp.zeros_like(state_ref)

    ext_ref[pl.ds(0, HALO), :] = jnp.where(blk > 0, halo_ref[...], 0.0)
    ext_ref[pl.ds(HALO, size), :] = proj_ref[:, :conv_width]
    pre_ref[...] = conv_rows(ext_ref, taps_ref, size)
    pos = blk * size + lax.broadcasted_iota(jnp.int32, (size, 1), 0)
    mask_col = (pos < len_ref[slot]).astype(f32)
    small = proj_ref[:, small_at : small_at + 128]
    _, _, cum, beta = small_terms(small, par_ref[0:1, :], par_ref[1:2, :], mask_col, heads, size)
    cum_t = cum.T
    rows = lax.broadcasted_iota(jnp.int32, (size, size), 0)
    cols = lax.broadcasted_iota(jnp.int32, (size, size), 1)
    hs = range(heads)
    scale = kw ** (-0.5)
    q, k, v = [], [], []
    for h in hs:
        _, _, u = unit_rows(pre_ref[:, h * kw : (h + 1) * kw], 1.0)
        q.append((u * scale).astype(bf16))
        _, _, u = unit_rows(pre_ref[:, (heads + h) * kw : (heads + h + 1) * kw], 1.0)
        k.append(u)
        pv = pre_ref[:, 2 * heads * kw + h * vw : 2 * heads * kw + (h + 1) * vw]
        v.append(pv * sigmoid(pv))
    kl = [a.astype(bf16) for a in k]
    cc = [cum[:, h : h + 1] for h in hs]
    cr = [cum_t[h : h + 1, :] for h in hs]
    bc = [beta[:, heads + h : heads + h + 1] for h in hs]
    dec = [jnp.where(rows >= cols, jnp.exp(jnp.minimum(cc[h] - cr[h], 0.0)), 0.0) for h in hs]
    kk = [contract(kl[h], kl[h], 1, 1) for h in hs]
    qk = [contract(q[h], kl[h], 1, 1) for h in hs]
    a = [jnp.where(rows > cols, bc[h] * kk[h] * dec[h], 0.0) for h in hs]
    inv = block_inverse(a, base)
    sl = [state_ref[h].astype(bf16) for h in hs]
    ks = [contract(kl[h], sl[h], 1, 0) for h in hs]
    qs = [contract(q[h], sl[h], 1, 0) for h in hs]
    ec = [jnp.exp(cc[h]) for h in hs]
    rhs = [bc[h] * (v[h] - ec[h] * ks[h]) for h in hs]
    new = [dot_split(two_terms(inv[h]), two_terms(rhs[h]), 1, 0) for h in hs]
    new2 = [two_terms(new[h]) for h in hs]
    o = [ec[h] * qs[h] + dot_split(two_terms(qk[h] * dec[h]), new2[h], 1, 0) for h in hs]
    for h in hs:
        s_ref[0, h] = state_ref[h]
        last = cum[size - 1 : size, h : h + 1]
        kel = (k[h] * jnp.exp(last - cc[h])).astype(bf16)
        state_ref[h] = jnp.exp(last) * state_ref[h] + contract(kel, new2[h][0], 0, 0)
        x_ref[:, h * size : (h + 1) * size] = inv[h]
        new_ref[:, h * vw : (h + 1) * vw] = new[h]
        o_ref[:, h * vw : (h + 1) * vw] = o[h]
        r = lax.rsqrt(jnp.mean(o[h] * o[h], axis=-1, keepdims=True) + 1e-05)
        g = proj_ref[:, small_at + LANES + h * vw : small_at + LANES + (h + 1) * vw]
        gated_ref[:, h * vw : (h + 1) * vw] = (
            o[h] * r * gain_ref[...] * (g * sigmoid(g))
        ).astype(bf16)


def mixer_backward_kernel(
    heads, kw, vw, size, base,
    len_ref, at_ref, proj_ref, halo_ref, taps_ref, par_ref, do_ref, dhead_ref, x_ref, new_ref, s_ref,
    dproj_ref, dmix_ref, dtaps_ref, dpar_ref,
    ext_ref, pre_ref, dext_ref, dstate_ref,
):
    slot, step = pl.program_id(0), pl.program_id(1)
    blk = pl.num_programs(1) - 1 - step
    conv_width = heads * (2 * kw + vw)
    small_at = conv_width
    count = taps_ref.shape[0]

    @pl.when((step == 0) & (slot == 0))
    def _():
        dtaps_ref[...] = jnp.zeros_like(dtaps_ref)
        dpar_ref[...] = jnp.zeros_like(dpar_ref)

    @pl.when(step == 0)
    def _():
        dstate_ref[...] = jnp.zeros_like(dstate_ref)
        dext_ref[pl.ds(0, HALO), :] = jnp.zeros((HALO, conv_width), f32)

    dext_ref[pl.ds(size, HALO), :] = dext_ref[pl.ds(0, HALO), :]
    ext_ref[pl.ds(0, HALO), :] = jnp.where(blk > 0, halo_ref[...], 0.0)
    ext_ref[pl.ds(HALO, size), :] = proj_ref[:, :conv_width]
    pre_ref[...] = conv_rows(ext_ref, taps_ref, size)
    pos = blk * size + lax.broadcasted_iota(jnp.int32, (size, 1), 0)
    mask_col = (pos < len_ref[slot]).astype(f32)
    small = proj_ref[:, small_at : small_at + 128]
    z, decay, cum, beta = small_terms(small, par_ref[0:1, :], par_ref[1:2, :], mask_col, heads, size)
    cum_t = cum.T
    rows = lax.broadcasted_iota(jnp.int32, (size, size), 0)
    cols = lax.broadcasted_iota(jnp.int32, (size, size), 1)
    hs = range(heads)
    scale = kw ** (-0.5)
    at_q = [slice(h * kw, (h + 1) * kw) for h in hs]
    at_k = [slice((heads + h) * kw, (heads + h + 1) * kw) for h in hs]
    at_v = [slice(2 * heads * kw + h * vw, 2 * heads * kw + (h + 1) * vw) for h in hs]
    at_o = [slice(h * vw, (h + 1) * vw) for h in hs]
    cc = [cum[:, h : h + 1] for h in hs]
    cr = [cum_t[h : h + 1, :] for h in hs]
    bc = [beta[:, heads + h : heads + h + 1] for h in hs]
    ec = [jnp.exp(cc[h]) for h in hs]
    do = [do_ref[:, at_o[h]] for h in hs]
    q_terms = [unit_rows(pre_ref[:, at_q[h]], 1.0) for h in hs]
    k_terms = [unit_rows(pre_ref[:, at_k[h]], 1.0) for h in hs]
    q = [terms[2] * scale for terms in q_terms]
    k = [terms[2] for terms in k_terms]
    ql = [u.astype(bf16) for u in q]
    kl = [u.astype(bf16) for u in k]
    dec = [jnp.where(rows >= cols, jnp.exp(jnp.minimum(cc[h] - cr[h], 0.0)), 0.0) for h in hs]
    kk = [contract(kl[h], kl[h], 1, 1) for h in hs]
    qk = [contract(ql[h], kl[h], 1, 1) for h in hs]
    pm = [qk[h] * dec[h] for h in hs]
    sl = [s_ref[0, h].astype(bf16) for h in hs]
    tl = [dstate_ref[h].astype(bf16) for h in hs]
    ks = [contract(kl[h], sl[h], 1, 0) for h in hs]
    qs = [contract(ql[h], sl[h], 1, 0) for h in hs]
    new2 = [two_terms(new_ref[:, at_o[h]]) for h in hs]
    do2 = [two_terms(do[h]) for h in hs]
    last = [cum[size - 1 : size, h : h + 1] for h in hs]
    el = [jnp.exp(last[h] - cc[h]) for h in hs]
    kel = [(k[h] * el[h]).astype(bf16) for h in hs]
    dpm = [dot_split(do2[h], new2[h], 1, 1) for h in hs]
    dnew = [dot_split(two_terms(pm[h]), do2[h], 0, 0) + contract(kel[h], tl[h], 1, 0) for h in hs]
    drhs = [dot_split(two_terms(x_ref[:, h * size : (h + 1) * size]), two_terms(dnew[h]), 0, 0) for h in hs]
    da = [-dot_split(two_terms(drhs[h]), new2[h], 1, 1) for h in hs]
    dkel = [contract(new2[h][0], tl[h], 1, 1) for h in hs]
    dcol, dbeta = [], []
    dq, dk, edo, edz = [], [], [], []
    lastrow = (lax.broadcasted_iota(jnp.int32, (size, 1), 0) == size - 1).astype(f32)
    for h in hs:
        pv = pre_ref[:, at_v[h]]
        sv = sigmoid(pv)
        zz = pv * sv - ec[h] * ks[h]
        dz = bc[h] * drhs[h]
        db = jnp.sum(drhs[h] * zz, axis=-1, keepdims=True)
        dext_ref[pl.ds(0, size), at_v[h]] = dz * (sv * (1.0 + pv * (1.0 - sv)))
        edo.append((ec[h] * do[h]).astype(bf16))
        edz.append((-ec[h] * dz).astype(bf16))
        dec_col = jnp.sum(do[h] * qs[h] - dz * ks[h], axis=-1, keepdims=True)
        dam = jnp.where(rows > cols, da[h], 0.0)
        dpmm = jnp.where(rows >= cols, dpm[h], 0.0)
        kd = kk[h] * dec[h]
        db = db + jnp.sum(dam * kd, axis=-1, keepdims=True)
        dspread = dpmm * pm[h] + dam * (bc[h] * kd)
        dqk = (dpmm * dec[h]).astype(bf16)
        dkk = (dam * (bc[h] * dec[h])).astype(bf16)
        d_el = jnp.sum(dkel[h] * k[h], axis=-1, keepdims=True) * el[h]
        d_keep = jnp.sum(jnp.sum(dstate_ref[h] * s_ref[0, h], axis=-1, keepdims=True), axis=0, keepdims=True)
        d_last = d_keep * jnp.exp(last[h]) + jnp.sum(d_el, axis=0, keepdims=True)
        col = jnp.sum(dspread, axis=-1, keepdims=True) + dec_col * ec[h] - d_el + lastrow * d_last
        row = jnp.sum(dspread, axis=0, keepdims=True)
        dcol.append((col, row))
        dbeta.append(db)
        dq.append(contract(edo[h], sl[h], 1, 1) + contract(dqk, kl[h], 1, 0))
        dk.append(
            contract(edz[h], sl[h], 1, 1)
            + dkel[h] * el[h]
            + contract(dqk, ql[h], 0, 0)
            + contract(dkk, kl[h], 1, 0)
            + contract(dkk, kl[h], 0, 0)
        )
    for h in hs:
        dstate_ref[h] = (
            jnp.exp(last[h]) * dstate_ref[h]
            + contract(ql[h], edo[h], 0, 0)
            + contract(kl[h], edz[h], 0, 0)
        )
        for at, du, terms in (
            (at_q[h], dq[h] * scale, q_terms[h]),
            (at_k[h], dk[h], k_terms[h]),
        ):
            pre = pre_ref[:, at]
            sig, r, u = terms
            dy = r * (du - u * jnp.sum(u * du, axis=-1, keepdims=True))
            dext_ref[pl.ds(0, size), at] = dy * (sig * (1.0 + pre * (1.0 - sig)))
    lanes = lax.broadcasted_iota(jnp.int32, (size, 128), 1)
    subs = lax.broadcasted_iota(jnp.int32, (128, size), 0)
    dcum = jnp.zeros((size, 128), f32)
    drow = jnp.zeros((128, size), f32)
    dbeta_all = jnp.zeros((size, 128), f32)
    for h in hs:
        dcum = jnp.where(lanes == h, dcol[h][0], dcum)
        drow = jnp.where(subs == h, dcol[h][1], drow)
        dbeta_all = jnp.where(lanes == heads + h, dbeta[h], dbeta_all)
    dcum = dcum - drow.T
    triu = (rows <= cols).astype(bf16)
    hi, lo = two_terms(dcum)
    ddecay = contract(triu, hi, 1, 0) + contract(triu, lo, 1, 0)
    dz = ddecay * (-jnp.exp(par_ref[0:1, :])) * sigmoid(z)
    dpar_ref[0:1, :] += jnp.sum(ddecay * decay, axis=0, keepdims=True)
    dpar_ref[1:2, :] += jnp.sum(dz, axis=0, keepdims=True)
    sb = sigmoid(small)
    dsmall = dz + dbeta_all * mask_col * sb * (1.0 - sb)
    dproj_ref[:, small_at : small_at + LANES] = dsmall.astype(bf16)
    dmix_ref[:, small_at : small_at + LANES] = dsmall.astype(bf16)
    dproj_ref[:, small_at + LANES :] = dhead_ref[...]
    dpre = dext_ref[pl.ds(0, size), :]
    total = None
    for j in range(count):
        back = dext_ref[pl.ds(count - 1 - j, size), :] * taps_ref[pl.ds(j, 1), :]
        total = back if total is None else total + back
        seen = ext_ref[pl.ds(HALO - count + 1 + j, size), :]
        dtaps_ref[pl.ds(j, 1), :] += jnp.sum(dpre * seen, axis=0, keepdims=True)
    dproj_ref[:, :conv_width] = total.astype(bf16)
    dmix_ref[:, :conv_width] = total.astype(bf16)


def mixer_specs(heads, kw, vw, size, blocks, width, taps, per_owner, order):
    conv_width = heads * (2 * kw + vw)
    per = size // HALO

    def place(index, at_ref):
        return at_ref[index // per_owner] * per_owner + lax.rem(index, per_owner)

    def at(s, b, len_ref, at_ref):
        return place(s * blocks + order(b), at_ref), 0

    def before(s, b, len_ref, at_ref):
        index = jnp.maximum(s * blocks + order(b) - 1, 0)
        return place(index, at_ref) * per + per - 1, 0

    return dict(
        proj=pl.BlockSpec((size, width), at),
        mix=pl.BlockSpec((size, conv_width + LANES), at),
        halo=pl.BlockSpec((HALO, conv_width), before),
        taps=pl.BlockSpec((taps, conv_width), lambda s, b, *_: (0, 0)),
        par=pl.BlockSpec((8, LANES), lambda s, b, *_: (0, 0)),
        gain=pl.BlockSpec((1, vw), lambda s, b, *_: (0, 0)),
        value=pl.BlockSpec((size, heads * vw), at),
        inv=pl.BlockSpec((size, heads * size), at),
        state=pl.BlockSpec((1, heads, kw, vw), lambda s, b, *_: (s * blocks + order(b), 0, 0, 0)),
    )


def mixer_forward(lengths, place, proj, taps, par, gain, heads, kw, vw, size=128, base=16):
    slots = lengths.shape[0]
    rows, width = proj.shape
    blocks = rows // slots // size
    per_owner = rows // size // place.shape[0]
    sp = mixer_specs(
        heads, kw, vw, size, blocks, width, taps.shape[0], per_owner, lambda b: b
    )
    conv_width = heads * (2 * kw + vw)
    return pl.pallas_call(
        functools.partial(mixer_forward_kernel, heads, kw, vw, size, base),
        grid_spec=pltpu.PrefetchScalarGridSpec(
            num_scalar_prefetch=2,
            grid=(slots, blocks),
            in_specs=[sp[n] for n in ("proj", "halo", "taps", "par", "gain")],
            out_specs=[sp[n] for n in ("value", "value", "inv", "value", "state")],
            scratch_shapes=[
                pltpu.VMEM((size + HALO, conv_width), f32),
                pltpu.VMEM((size, conv_width), f32),
                pltpu.VMEM((heads, kw, vw), f32),
            ],
        ),
        out_shape=[
            jax.ShapeDtypeStruct((rows, heads * vw), bf16),
            jax.ShapeDtypeStruct((rows, heads * vw), f32),
            jax.ShapeDtypeStruct((rows, heads * size), f32),
            jax.ShapeDtypeStruct((rows, heads * vw), f32),
            jax.ShapeDtypeStruct((slots * blocks, heads, kw, vw), f32),
        ],
        compiler_params=pltpu.CompilerParams(dimension_semantics=("arbitrary", "arbitrary")),
        cost_estimate=pl.CostEstimate(
            flops=rows * heads * 8000000, bytes_accessed=rows * width * 12, transcendentals=rows * width
        ),
        name="mixer_forward",
    )(lengths, place, proj, proj, taps, par, gain)


def mixer_backward(
    lengths, place, proj, taps, par, d_out, d_head, inv, new, state, heads, kw, vw, size=128, base=16
):
    slots = lengths.shape[0]
    rows, width = proj.shape
    blocks = rows // slots // size
    per_owner = rows // size // place.shape[0]
    sp = mixer_specs(
        heads, kw, vw, size, blocks, width, taps.shape[0], per_owner, lambda b: blocks - 1 - b
    )
    conv_width = heads * (2 * kw + vw)
    return pl.pallas_call(
        functools.partial(mixer_backward_kernel, heads, kw, vw, size, base),
        grid_spec=pltpu.PrefetchScalarGridSpec(
            num_scalar_prefetch=2,
            grid=(slots, blocks),
            in_specs=[
                sp[n]
                for n in ("mix", "halo", "taps", "par", "value", "value", "inv", "value", "state")
            ],
            out_specs=[sp[n] for n in ("proj", "mix", "taps", "par")],
            scratch_shapes=[
                pltpu.VMEM((size + HALO, conv_width), f32),
                pltpu.VMEM((size, conv_width), f32),
                pltpu.VMEM((size + HALO, conv_width), f32),
                pltpu.VMEM((heads, kw, vw), f32),
            ],
        ),
        out_shape=[
            jax.ShapeDtypeStruct((rows, width), bf16),
            jax.ShapeDtypeStruct((rows, conv_width + LANES), bf16),
            jax.ShapeDtypeStruct(taps.shape, f32),
            jax.ShapeDtypeStruct((8, LANES), f32),
        ],
        compiler_params=pltpu.CompilerParams(dimension_semantics=("arbitrary", "arbitrary")),
        cost_estimate=pl.CostEstimate(
            flops=rows * heads * 12000000, bytes_accessed=rows * width * 12, transcendentals=rows * width
        ),
        name="mixer_backward",
    )(lengths, place, proj, proj, taps, par, d_out, d_head, inv, new, state)


def head_backward_kernel(heads, vw, gain_ref, d_ref, o_ref, head_ref, dout_ref, dhead_ref, dgain_ref):
    @pl.when(pl.program_id(0) == 0)
    def _():
        dgain_ref[...] = jnp.zeros_like(dgain_ref)

    gain = gain_ref[...]
    total = jnp.zeros_like(gain)
    for h in range(heads):
        at = slice(h * vw, (h + 1) * vw)
        g = head_ref[:, at]
        sig = sigmoid(g)
        silu = g * sig
        o = o_ref[:, at]
        r = lax.rsqrt(jnp.mean(o * o, axis=-1, keepdims=True) + 1e-05)
        unit = o * r
        d = d_ref[:, at]
        both = d * unit
        dhead_ref[:, at] = (both * gain * (sig * (1.0 + g * (1.0 - sig)))).astype(bf16)
        total = total + jnp.sum(both * silu, axis=0, keepdims=True)
        dn = d * gain * silu
        dout_ref[:, at] = r * (dn - unit * jnp.mean(unit * dn, axis=-1, keepdims=True))
    dgain_ref[...] += total


def head_backward(gain, d_gated, o, proj, heads, vw, size=256):
    rows, width = o.shape
    size = min(size, rows)
    block = pl.BlockSpec((size, width), lambda i: (i, 0))
    row = pl.BlockSpec((1, vw), lambda i: (0, 0))
    start = proj.shape[1] - width
    cols = pl.BlockSpec((pl.Element(size), pl.Element(width)), lambda i: (i * size, start))
    return pl.pallas_call(
        functools.partial(head_backward_kernel, heads, vw),
        grid=(rows // size,),
        in_specs=[row, block, block, cols],
        out_specs=[block, block, row],
        out_shape=[
            jax.ShapeDtypeStruct((rows, width), f32),
            jax.ShapeDtypeStruct((rows, width), bf16),
            jax.ShapeDtypeStruct((1, vw), f32),
        ],
        cost_estimate=pl.CostEstimate(
            flops=rows * width * 30, bytes_accessed=rows * width * 18, transcendentals=rows * width
        ),
        name="head_backward",
    )(gain, d_gated, o, proj)


def turn(value_in):
    size = lax.axis_size("tensor")
    return lax.ppermute(value_in, "tensor", [(i, (i + 1) % size) for i in range(size)])


def after(value_in, *others):
    return lax.optimization_barrier((value_in,) + others)[0]


def ring_gather(piece):
    pieces = [piece]
    for _ in range(lax.axis_size("tensor") - 1):
        pieces.append(turn(pieces[-1]))
    return pieces[1:] + pieces[:1]


def ring_scatter(pieces):
    total = None
    for piece in pieces[:-1]:
        send = piece.astype(f32)
        if total is not None:
            send = send + total.astype(f32)
        total = turn(send.astype(bf16))
    return pieces[-1].astype(f32) + total.astype(f32)


def cube_pick(array, bit, dim):
    me = lax.axis_index("dp")
    mine = lax.rem(me // (1 << bit), 2)
    keep = lax.dynamic_index_in_dim(array, mine, dim, keepdims=False)
    return keep, lax.dynamic_index_in_dim(array, 1 - mine, dim, keepdims=False)


def cube_swap(kept, bit):
    pairs = [(i, i ^ (1 << bit)) for i in range(lax.axis_size("dp"))]
    return kept[0], lax.ppermute(kept[1], "dp", pairs)


def joined(pair):
    return (pair[0].astype(f32) + pair[1].astype(f32)).astype(bf16)


def cube_ready(value_in):
    if lax.axis_size("dp") != 8:
        return (value_in,)
    return cube_pick(value_in.reshape(2, 2, 2, value_in.shape[0] // 8, -1), 0, 2)


def cube_first(held):
    return held if len(held) == 1 else cube_swap(held, 0)


def cube_second(held, cut):
    if len(held) == 1:
        return held
    whole = joined(held)
    return cube_swap(cube_pick(whole[..., :cut], 1, 1), 1) + cube_swap(
        cube_pick(whole[..., cut:], 2, 0), 2
    )


def cube_third(held):
    if len(held) == 1:
        return held
    return cube_swap(cube_pick(joined(held[:2]), 2, 0), 2) + cube_swap(
        cube_pick(joined(held[2:]), 1, 0), 1
    )


def cube_columns(held, cut, lo, hi):
    if len(held) == 1:
        return lax.psum_scatter(held[0][:, lo:hi], "dp", scatter_dimension=0, tiled=True).astype(f32)
    pair, lo, hi = (held[:2], lo, hi) if hi <= cut else (held[2:], lo - cut, hi - cut)
    return pair[0][:, lo:hi].astype(f32) + pair[1][:, lo:hi].astype(f32)


def meet(*values):
    return lax.optimization_barrier(values)


def cube_sum(value_in, axis):
    size = lax.axis_size(axis)
    if size & (size - 1):
        return lax.psum(value_in, axis)
    bit = 1
    while bit < size:
        value_in = value_in + lax.ppermute(value_in, axis, [(i, i ^ bit) for i in range(size)])
        bit *= 2
    return value_in


def rms_rows(value_in):
    return lax.rsqrt(jnp.mean(value_in * value_in, axis=-1, keepdims=True) + 1e-05)


def body(
    block_in,
    slot_lengths,
    attn_gain,
    query_weight,
    key_weight,
    value_weight,
    output_gate,
    decay_weight,
    beta_weight,
    conv_weight,
    decay_log,
    step_bias,
    head_gain,
    out_weight,
    ffn_gain,
    gate_weight,
    up_weight,
    down_weight,
    out_grad,
):
    tensor_size = lax.axis_size("tensor")
    tensor_rank = lax.axis_index("tensor")
    local_rows = block_in.shape[0]
    group_rows = local_rows * tensor_size
    slots_here = slot_lengths.shape[0]
    slot_length = group_rows // slots_here
    heads_here = decay_weight.shape[1]
    total_heads = decay_log.shape[0]
    key_channels = query_weight.shape[1]
    value_channels = value_weight.shape[1]
    key_width = key_channels // heads_here
    value_width = value_channels // heads_here
    model = attn_gain.shape[0]
    ring = range(tensor_size)
    row_of = tensor_rank * local_rows + jnp.arange(local_rows, dtype=jnp.int32)
    local_mask = (
        lax.rem(row_of, slot_length) < jnp.take(slot_lengths, row_of // slot_length)
    ).astype(f32)[:, None]
    place = lax.rem(
        tensor_rank - jnp.arange(tensor_size, dtype=jnp.int32) + 2 * tensor_size - 1, tensor_size
    )
    query_start = tensor_rank * key_channels
    key_start = total_heads * key_width + tensor_rank * key_channels
    value_start = 2 * total_heads * key_width + tensor_rank * value_channels
    taps = jnp.concatenate(
        [
            lax.dynamic_slice_in_dim(conv_weight, query_start, key_channels, 1),
            lax.dynamic_slice_in_dim(conv_weight, key_start, key_channels, 1),
            lax.dynamic_slice_in_dim(conv_weight, value_start, value_channels, 1),
        ],
        axis=1,
    )
    rate_local = lax.dynamic_slice_in_dim(decay_log, tensor_rank * heads_here, heads_here)
    bias_local = lax.dynamic_slice_in_dim(step_bias, tensor_rank * heads_here, heads_here)
    par = jnp.pad(jnp.stack([rate_local, bias_local]), ((0, 6), (0, LANES - heads_here)))

    small_local = jnp.concatenate([decay_weight, beta_weight], axis=1)
    mix_local = jnp.concatenate(
        [
            query_weight,
            key_weight,
            value_weight,
            jnp.pad(small_local, ((0, 0), (0, LANES - 2 * heads_here))),
            output_gate,
        ],
        axis=1,
    )
    mix_full = lax.all_gather(mix_local, "dp", axis=0, tiled=True)
    block_pieces = ring_gather(block_in)
    out_full = lax.all_gather(out_weight, "dp", axis=1, tiled=True)
    gate_full = lax.all_gather(gate_weight, "dp", axis=0, tiled=True)
    up_full = lax.all_gather(up_weight, "dp", axis=0, tiled=True)
    down_full = lax.all_gather(down_weight, "dp", axis=1, tiled=True)

    def owners(grad_piece, dim):
        return lax.psum_scatter(grad_piece, "dp", scatter_dimension=dim, tiled=True).astype(f32)

    units, mixer_pieces = [], []
    for piece in block_pieces:
        piece = piece.astype(f32)
        units.append(piece * rms_rows(piece))
        mixer_pieces.append((units[-1] * attn_gain).astype(bf16))
    out_masked = out_grad.astype(f32) * local_mask
    mixer_rows = jnp.concatenate(mixer_pieces)
    proj = jnp.dot(mixer_rows, mix_full, preferred_element_type=f32)
    back_own = after(out_masked.astype(bf16), block_pieces[-2])
    back_pieces = [turn(back_own)]
    proj = after(proj, back_pieces[0])
    back_pieces.append(turn(after(back_pieces[0], proj)))
    gated, o, inv, new, state = mixer_forward(
        slot_lengths, place, proj, taps, par, head_gain[None, :], heads_here, key_width, value_width
    )
    gated = after(gated, back_pieces[1])
    for _ in range(3, tensor_size):
        back_pieces.append(turn(back_pieces[-1]))
    back_pieces.append(back_own)

    def split(rows_in):
        return [rows_in[i * local_rows : (i + 1) * local_rows] for i in ring]

    mixer_out = ring_scatter(split(jnp.dot(gated, out_full, preferred_element_type=f32)))
    hidden = block_in.astype(f32) + mixer_out
    hidden_scale = rms_rows(hidden)
    hidden_unit = hidden * hidden_scale

    ffn_pieces = ring_gather((hidden_unit * ffn_gain).astype(bf16))
    inner_pieces, gate_pieces, up_pieces, part_pieces = [], [], [], []
    for piece, back in zip(ffn_pieces, back_pieces):
        gate_act = jnp.dot(piece, gate_full, preferred_element_type=f32)
        up_act = jnp.dot(piece, up_full, preferred_element_type=f32)
        gate_sig = jax.nn.sigmoid(gate_act)
        gate_silu = gate_act * gate_sig
        inner_pieces.append((gate_silu * up_act).astype(bf16))
        d_inner = contract(back, down_full, 1, 1)
        d_gate = (d_inner * up_act * gate_sig * (1.0 + gate_act * (1.0 - gate_sig))).astype(bf16)
        d_up = (d_inner * gate_silu).astype(bf16)
        gate_pieces.append(d_gate)
        up_pieces.append(d_up)
        part_pieces.append(contract(d_gate, gate_full, 1, 1) + contract(d_up, up_full, 1, 1))
    d_ffn_in = ring_scatter(part_pieces)
    grad_ffn_gain = jnp.sum(d_ffn_in * hidden_unit, axis=0)
    dn = d_ffn_in * ffn_gain
    d_hidden = out_masked + hidden_scale * (
        dn - hidden_unit * jnp.mean(dn * hidden_unit, axis=-1, keepdims=True)
    )
    mix_own = d_hidden.astype(bf16)
    ffn_rows = jnp.concatenate([after(p, mix_own) for p in ffn_pieces])
    inner_rows = jnp.concatenate([after(p, mix_own) for p in inner_pieces])

    hop, ffn_out_part, grad_gate = meet(
        turn(mix_own),
        jnp.dot(inner_rows, down_full, preferred_element_type=f32),
        contract(ffn_rows, jnp.concatenate(gate_pieces), 0, 0).astype(bf16),
    )
    mix_pieces = [hop]
    sum_gate = owners(grad_gate, 0)
    up_rows = jnp.concatenate([after(p, hop) for p in up_pieces])
    hop, grad_up, grad_down = meet(
        turn(hop),
        contract(ffn_rows, up_rows, 0, 0).astype(bf16),
        contract(after(inner_rows, hop), jnp.concatenate(back_pieces), 0, 0).astype(bf16),
    )
    mix_pieces.append(hop)
    sum_up, sum_down = owners(grad_up, 0), owners(grad_down, 1)
    out_pieces = split(ffn_out_part)
    out_total = turn(after(out_pieces[0].astype(bf16), hop))
    for _ in range(3, tensor_size):
        hop = turn(hop)
        mix_pieces.append(hop)
    mix_back, out_total = meet(jnp.concatenate(mix_pieces + [mix_own]), out_total)

    d_gated = contract(mix_back, out_full, 1, 1)
    d_out, d_head, grad_head_gain = head_backward(
        head_gain[None, :], d_gated, o, proj, heads_here, value_width
    )
    out_total = turn((after(out_pieces[1], mix_back) + out_total.astype(f32)).astype(bf16))
    grad_out = contract(mix_back, gated, 0, 0).astype(bf16)
    d_out, out_total, out_held = meet(d_out, out_total, cube_ready(grad_out))
    out_held = cube_first(out_held)
    for index in range(2, tensor_size - 1):
        out_total = turn((after(out_pieces[index], d_out) + out_total.astype(f32)).astype(bf16))
    d_proj, d_mix, d_taps, d_par = mixer_backward(
        slot_lengths, place, proj, taps, par, d_out, d_head, inv, new, state,
        heads_here, key_width, value_width,
    )
    cut = 2 * local_rows
    d_proj, out_total, out_held = meet(d_proj, out_total, out_held)
    early = contract(d_proj[:cut], mix_full, 1, 1).astype(bf16)
    first, second = meet(early[:local_rows], early[local_rows:])
    d_mix, d_head = after(d_mix, first), after(d_head, first)
    mix_cut, out_cut = 2 * key_channels, value_channels // 2
    total, mix_held, grad_head, out_held = meet(
        turn(first),
        cube_ready(contract(mixer_rows, d_mix, 0, 0).astype(bf16)),
        contract(mixer_rows, d_head, 0, 0).astype(bf16),
        cube_second(out_held, out_cut),
    )
    sum_head = owners(grad_head, 0)
    rest = contract(after(d_proj, total)[cut:], mix_full, 1, 1).astype(bf16)
    total, mix_held, rest, out_held = meet(
        turn((second.astype(f32) + total.astype(f32)).astype(bf16)),
        cube_first(mix_held),
        rest,
        cube_third(out_held),
    )
    mixer_parts = [first, second] + [
        rest[i * local_rows : (i + 1) * local_rows] for i in range(tensor_size - 2)
    ]
    mix_held = cube_second(mix_held, mix_cut)
    sum_out = jnp.concatenate(
        [
            cube_columns(out_held, out_cut, 0, out_cut),
            cube_columns(out_held, out_cut, out_cut, value_channels),
        ],
        axis=1,
    ).T
    grad_attn_gain = sum(
        jnp.sum(p.astype(f32) * u, axis=0) for p, u in zip(mixer_parts, units)
    )
    for index in range(2, tensor_size - 1):
        total = turn((mixer_parts[index].astype(f32) + total.astype(f32)).astype(bf16))
    total, mix_held, sum_head = meet(total, mix_held, sum_head)
    mix_held = cube_third(mix_held)
    d_mixer_in = mixer_parts[-1].astype(f32) + total.astype(f32)
    ffn_out = out_pieces[-1] + out_total.astype(f32)
    block_out = (local_mask * (hidden + ffn_out)).astype(bf16)
    block_scale = rms_rows(block_in.astype(f32))
    unit = units[-1]
    dn = d_mixer_in * attn_gain
    grad_in = d_hidden + block_scale * (dn - unit * jnp.mean(dn * unit, axis=-1, keepdims=True))

    shared = jnp.concatenate([grad_attn_gain, grad_ffn_gain, grad_head_gain[0]])
    packed = jnp.concatenate([d_taps.reshape(-1), d_par[:2].reshape(-1), shared])
    width = packed.shape[0]
    padded = -(-width // 1024) * 1024
    packed = jnp.pad(packed, (0, padded - width)).reshape(padded // LANES, LANES)
    table = jnp.stack(ring_gather(cube_sum(packed, "dp")))
    table = jnp.take(table, place, axis=0).reshape(tensor_size, padded)
    taps_all = table[:, : d_taps.size].reshape((tensor_size,) + d_taps.shape)
    cuts = (0, key_channels, 2 * key_channels, 2 * key_channels + value_channels)
    conv_grad = jnp.concatenate(
        [
            taps_all[:, :, lo:hi].transpose(1, 0, 2).reshape(d_taps.shape[0], -1)
            for lo, hi in zip(cuts[:-1], cuts[1:])
        ],
        axis=1,
    )
    at = d_taps.size
    rate_grad = table[:, at : at + heads_here].reshape(-1)
    at += LANES
    bias_grad = table[:, at : at + heads_here].reshape(-1)
    at += LANES
    totals = jnp.sum(table[:, at : at + shared.shape[0]], axis=0)
    sum_small = cube_columns(mix_held, mix_cut, cuts[-1], cuts[-1] + LANES)
    return (
        block_out,
        grad_in,
        totals[:model],
        cube_columns(mix_held, mix_cut, 0, cuts[1]),
        cube_columns(mix_held, mix_cut, cuts[1], cuts[2]),
        cube_columns(mix_held, mix_cut, cuts[2], cuts[3]),
        sum_head,
        sum_small[:, :heads_here],
        sum_small[:, heads_here : 2 * heads_here],
        conv_grad,
        rate_grad,
        bias_grad,
        totals[2 * model :],
        sum_out,
        totals[model : 2 * model],
        sum_gate,
        sum_up,
        sum_down,
    )


def solution(mesh):
    rows = P(("dp", "tensor"), None)
    wide = P("dp", "tensor")
    tall = P("tensor", "dp")
    return jax.shard_map(
        body,
        mesh=mesh,
        in_specs=(
            rows, P("dp"), P(), wide, wide, wide, wide, wide, wide,
            P(), P(), P(), P(), tall, P(), wide, wide, tall, rows,
        ),
        out_specs=(
            rows, rows, P(), wide, wide, wide, wide, wide, wide,
            P(), P(), P(), P(), tall, P(), wide, wide, tall,
        ),
        check_vma=False,
    )
```
